768 devices in a mesh: seq: 48 (over x_lo, z, core), head: 16 (over x_hi, y).
Axes of the slice: x: 4 (x_hi: 2, x_lo: 2; x = x_hi * 2 + x_lo), y: 8, z: 12, core: 2. Of those that a mesh axis runs over, the one named last changes fastest.
Arguments:
- query_rows: bfloat16 [30720, 8192], P(('seq', 'head')), may hold values from -6 to 6
- rotated_key_rows: bfloat16 [30720, 1024], P(('seq', 'head')), may hold values from -6 to 6
- value_row_matrix: bfloat16 [30720, 1024], P(('seq', 'head')), may hold values from -6 to 6
- group_assign: int32 [64], replicated, may hold values from 0 to 63, each once
- vertical_blocks: int32 [64, 4], replicated, may hold values from 0 to 239
- slash_offsets: int32 [64, 3], replicated, may hold values from 0 to 5, as said below
Outputs:
- attended: bfloat16 [30720, 8192], P(('seq', 'head'))
The draws below stay inside these ranges and needn't reach their ends.
Inputs may be any that keep to these rules, and one draw needn't show every extreme that they name: `slash_offsets`: each head's first offset is 0 and its offsets are distinct.
All inputs are finite; a program needn't handle non-finite values.
Results may differ from the reference program's by a relative error of at most 0.0045.
Values may be sent and summed in bfloat16 or wider, within the bound.
No kernel may reach another device: no remote copies, remote signals or barrier semaphores. Data moves between devices by JAX's collectives and lax.ppermute only.
A program may use at most 32 MiB of HBM per device.

```python
import math
import jax
import jax.numpy as jnp
from jax import lax

QUERY_HEADS = 64
KEY_VALUE_HEADS = 8
HEAD_SIZE = 128
BLOCK_TOKENS = 128
NV = 4
NS = 3
S_LOC = 640
SEQUENCE_TOKENS = 30720
NB = 240


def draw_query_rows(key, part):
    base_offset = jax.random.truncated_normal(jax.random.fold_in(key, 5), -6.0, 6.0, (SEQUENCE_TOKENS, QUERY_HEADS, HEAD_SIZE))
    return base_offset.reshape(SEQUENCE_TOKENS, QUERY_HEADS * HEAD_SIZE).astype(jnp.float32).astype(jnp.bfloat16)


def draw_rotated_key_rows(key, part):
    base_offset = jax.random.truncated_normal(jax.random.fold_in(key, 29), -6.0, 6.0, (SEQUENCE_TOKENS, KEY_VALUE_HEADS, HEAD_SIZE))
    return base_offset.reshape(SEQUENCE_TOKENS, KEY_VALUE_HEADS * HEAD_SIZE).astype(jnp.float32).astype(jnp.bfloat16)


def draw_slash_offsets(key, part):
    head_keys = jax.random.split(key, QUERY_HEADS)
    orders = jax.vmap(lambda single: jax.random.permutation(single, S_LOC // BLOCK_TOKENS))(head_keys) + 1
    leading = jnp.zeros((QUERY_HEADS, 1), jnp.int32)
    return jnp.concatenate([leading, orders[:, :NS - 1].astype(jnp.int32)], axis=1)


def set_ends(values, own_key, low, high):
    dims = values.shape
    spot = [jax.random.randint(jax.random.fold_in(own_key, axis), (), 0, dims[axis]) for axis in range(len(dims))]
    values = values.at[tuple(spot)].set(low)
    longest = dims.index(max(dims))
    spot[longest] = (spot[longest] + 1) % dims[longest]
    return values.at[tuple(spot)].set(high)


def shard_levels(own_key, extent, cuts, least, largest):
    def one(dim, parts):
        heights = jax.random.uniform(jax.random.fold_in(jax.random.fold_in(own_key, 6), dim), (parts,), jnp.float32, least / len(cuts), largest / len(cuts))
        return jnp.repeat(jnp.exp(heights), extent[dim] // parts).reshape((-1,) + (1,) * (len(extent) - dim - 1))

    factor_of = one(*cuts[0])
    for cut in cuts[1:]:
        factor_of = factor_of * one(*cut)
    return factor_of


def normal_values(rng, extent, spread, bound, cuts=(), kind=jnp.bfloat16):
    values = spread * jax.random.normal(rng, extent, jnp.float32)
    if cuts:
        values = values * shard_levels(rng, extent, cuts, -0.22, 0.18)
    return jnp.clip(values, -bound, bound).astype(kind)


def setup_inputs(seed: int = 0) -> dict:
    seeds = jax.random.split(jax.random.key(seed), 7)
    return {
        "query_rows": draw_query_rows(jax.random.fold_in(seeds[6], 71), 0),
        "rotated_key_rows": draw_rotated_key_rows(jax.random.fold_in(seeds[6], 71), 0),
        "value_row_matrix": normal_values(seeds[2], (SEQUENCE_TOKENS, KEY_VALUE_HEADS * HEAD_SIZE), 1.0, 6.0, ((0, 768),)),
        "group_assign": jax.random.permutation(seeds[3], QUERY_HEADS).astype(jnp.int32),
        "vertical_blocks": set_ends(jax.random.randint(seeds[4], (QUERY_HEADS, NV), 0, NB), jax.random.fold_in(seeds[4], 1), 0, NB - 1).astype(jnp.int32),
        "slash_offsets": draw_slash_offsets(jax.random.fold_in(seeds[6], 71), 0),
    }


def reference(query_rows, rotated_key_rows, value_row_matrix, group_assign, vertical_blocks, slash_offsets):
    count_of_blocks = SEQUENCE_TOKENS // BLOCK_TOKENS
    sharing_count = QUERY_HEADS // KEY_VALUE_HEADS
    query_blocks = query_rows.reshape(count_of_blocks, BLOCK_TOKENS, QUERY_HEADS, HEAD_SIZE)
    blocked_keys = rotated_key_rows.reshape(count_of_blocks, BLOCK_TOKENS, KEY_VALUE_HEADS, HEAD_SIZE)
    blocked_values = value_row_matrix.reshape(count_of_blocks, BLOCK_TOKENS, KEY_VALUE_HEADS, HEAD_SIZE)
    block_ids = jnp.arange(count_of_blocks, dtype=jnp.int32)
    within = jnp.arange(BLOCK_TOKENS, dtype=jnp.int32)
    earlier = jnp.arange(NV)[:, None] < jnp.arange(NV)[None, :]
    scaling = 1.0 / math.sqrt(HEAD_SIZE)
    width_count = NS + NV

    def attend_head(head):
        kv_head = head // sharing_count
        queries_head = lax.dynamic_index_in_dim(query_blocks, head, 2, keepdims=False)
        keys_head = lax.dynamic_index_in_dim(blocked_keys, kv_head, 2, keepdims=False)
        values_head = lax.dynamic_index_in_dim(blocked_values, kv_head, 2, keepdims=False)
        offsets = slash_offsets[head]
        verticals = vertical_blocks[head]
        slash_cand = block_ids[:, None] - offsets[None, :]
        slash_ok = slash_cand >= 0
        repeated = jnp.any((verticals[:, None] == verticals[None, :]) & earlier, axis=0)
        covered = jnp.any(block_ids[:, None, None] - verticals[None, :, None] == offsets[None, None, :], axis=2)
        vert_ok = (verticals[None, :] <= block_ids[:, None]) & jnp.logical_not(covered) & jnp.logical_not(repeated)[None, :]
        candidates = jnp.concatenate([jnp.maximum(slash_cand, 0), jnp.broadcast_to(verticals[None, :], (count_of_blocks, NV))], axis=1).astype(jnp.int32)
        cand_ok = jnp.concatenate([slash_ok, vert_ok], axis=1)
        gathered_keys = keys_head[candidates].reshape(count_of_blocks, width_count * BLOCK_TOKENS, HEAD_SIZE)
        gathered_values = values_head[candidates].reshape(count_of_blocks, width_count * BLOCK_TOKENS, HEAD_SIZE)
        key_pos = (candidates[:, :, None] * BLOCK_TOKENS + within[None, None, :]).reshape(count_of_blocks, width_count * BLOCK_TOKENS)
        query_pos = block_ids[:, None] * BLOCK_TOKENS + within[None, :]
        allowed = jnp.repeat(cand_ok, BLOCK_TOKENS, axis=1)[:, None, :] & (key_pos[:, None, :] <= query_pos[:, :, None])
        scores = jnp.einsum('nqd,nkd->nqk', queries_head.astype(jnp.float32), gathered_keys.astype(jnp.float32)) * scaling
        row_top = lax.optimization_barrier(jnp.max(jnp.where(allowed, scores, -jnp.inf), axis=2, keepdims=True))
        weights = jnp.where(allowed, jnp.exp(scores - row_top), 0.0)
        row_total = lax.optimization_barrier(jnp.sum(weights, axis=2, keepdims=True))
        rounded = lax.optimization_barrier(weights.astype(jnp.bfloat16))
        blended = jnp.einsum('nqk,nkd->nqd', rounded.astype(jnp.float32), gathered_values.astype(jnp.float32)) / row_total
        return blended.astype(jnp.bfloat16)
    per_slot = lax.map(attend_head, group_assign)
    return jnp.transpose(per_slot, (1, 2, 0, 3)).reshape(SEQUENCE_TOKENS, QUERY_HEADS * HEAD_SIZE)
```

```python
import functools
import math

import jax
import jax.numpy as jnp
from jax import lax
from jax.experimental import pallas as pl
from jax.experimental.pallas import tpu as pltpu
from jax.sharding import Mesh, PartitionSpec as P

QUERY_HEADS = 64
KEY_VALUE_HEADS = 8
HD = 128
BT = 128
NV = 4
NS = 3
GROUPS = 16
SLOTS = QUERY_HEADS // GROUPS
ROWS = 40
SEQ_ROWS = 640
LB = SEQ_ROWS // BT
CH = 16
SUB = 16
ALL = ("xl", "za", "zb", "c", "xh", "y")
SEQ = ("xl", "za", "zb", "c")
HEAD = ("xh", "y")
PART = ("xl", "zb", "c")
SCALE = 1.0 / math.sqrt(HD)
NEG = float("-inf")


def attend(meta, q_ref, kv_ref, prev_ref, vert_ref, o_ref, win, kc, vc):
    seq_place = meta[0]
    win[0:SEQ_ROWS, :] = prev_ref[...]
    win[SEQ_ROWS:, :] = kv_ref[...]
    causal = lax.broadcasted_iota(jnp.int32, (BT, BT), 0) >= lax.broadcasted_iota(
        jnp.int32, (BT, BT), 1
    )

    def one_head(h, carry):
        lane = pl.ds(pl.multiple_of(h * HD, HD), HD)
        offs = [meta[17 + h * NS + n] for n in range(NS)]
        verts = [meta[1 + h * NV + n] for n in range(NV)]
        for n in range(NV):
            rows = slice((NS + n) * BT, (NS + n + 1) * BT)
            for i in range(LB):
                kc[i, rows, :] = vert_ref[0:8, h * NV + n].reshape(BT, HD)
                vc[i, rows, :] = vert_ref[8:16, h * NV + n].reshape(BT, HD)
        for i in range(LB):
            block = seq_place * LB + i
            good = []
            for n in range(NS):
                at = pl.ds(pl.multiple_of((LB + i - offs[n]) * BT, BT), BT)
                rows = slice(n * BT, (n + 1) * BT)
                kc[i, rows, :] = win[at, 0:HD]
                vc[i, rows, :] = win[at, HD : 2 * HD]
                good.append(block - offs[n] >= 0)
            for n in range(NV):
                ok = verts[n] <= block
                for o in offs:
                    ok = ok & (block - verts[n] != o)
                for e in range(n):
                    ok = ok & (verts[n] != verts[e])
                good.append(ok)
            q = q_ref[i * BT : (i + 1) * BT, lane]
            s = (
                lax.dot_general(
                    q, kc[i], (((1,), (1,)), ((), ())), preferred_element_type=jnp.float32
                )
                * SCALE
            )
            parts = [jnp.where(causal, s[:, 0:BT], NEG)]
            for n in range(1, NS + NV):
                bias = jnp.where(good[n], 0.0, NEG)
                parts.append(s[:, n * BT : (n + 1) * BT] + bias)
            top = parts[0]
            for x in parts[1:]:
                top = jnp.maximum(top, x)
            top = jnp.max(top, axis=1, keepdims=True)
            ws = [jnp.exp(x - top) for x in parts]
            total = ws[0]
            for x in ws[1:]:
                total = total + x
            total = jnp.sum(total, axis=1, keepdims=True)
            w = jnp.concatenate([x.astype(jnp.bfloat16) for x in ws], axis=1)
            acc = jnp.dot(w, vc[i], preferred_element_type=jnp.float32)
            o_ref[i * BT : (i + 1) * BT, lane] = (acc / total).astype(jnp.bfloat16)
        return carry

    lax.fori_loop(0, SLOTS, one_head, 0)


def attention(meta, q, kv, prev, vert):
    vm = pl.BlockSpec(memory_space=pltpu.VMEM)
    return pl.pallas_call(
        attend,
        out_shape=jax.ShapeDtypeStruct((SEQ_ROWS, SLOTS * HD), jnp.bfloat16),
        in_specs=[pl.BlockSpec(memory_space=pltpu.SMEM), vm, vm, vm, vm],
        out_specs=vm,
        scratch_shapes=[
            pltpu.VMEM((2 * SEQ_ROWS, 2 * HD), jnp.bfloat16),
            pltpu.VMEM((LB, (NS + NV) * BT, HD), jnp.bfloat16),
            pltpu.VMEM((LB, (NS + NV) * BT, HD), jnp.bfloat16),
        ],
        name="attend",
    )(meta, q, kv, prev, vert)


def to_slots(assign, x_ref, o_ref):
    for k in range(QUERY_HEADS):
        a = assign[k]
        lane = pl.ds(pl.multiple_of((a % SLOTS) * HD, HD), HD)
        o_ref[:, k * HD : (k + 1) * HD] = x_ref[a // SLOTS, :, lane]


def place_slots(assign, x):
    vm = pl.BlockSpec(memory_space=pltpu.VMEM)
    return pl.pallas_call(
        to_slots,
        out_shape=jax.ShapeDtypeStruct((ROWS, QUERY_HEADS * HD), jnp.bfloat16),
        in_specs=[pl.BlockSpec(memory_space=pltpu.SMEM), vm],
        out_specs=vm,
        name="to_slots",
    )(assign, x)


def per_device(q_rows, k_rows, v_rows, group_assign, vertical_blocks, slash_offsets):
    group = lax.axis_index(HEAD)
    seq_place = lax.axis_index(SEQ)
    za = lax.axis_index("za")
    verts = lax.dynamic_slice_in_dim(vertical_blocks, group * SLOTS, SLOTS).reshape(-1)
    offs = lax.dynamic_slice_in_dim(slash_offsets, group * SLOTS, SLOTS).reshape(-1)

    kv = jnp.stack(
        [k_rows.reshape(ROWS, KEY_VALUE_HEADS, HD), v_rows.reshape(ROWS, KEY_VALUE_HEADS, HD)],
        axis=2,
    ).reshape(ROWS, KEY_VALUE_HEADS, 2 * HD)
    kv = jnp.repeat(jnp.transpose(kv, (1, 0, 2)), GROUPS // KEY_VALUE_HEADS, axis=0)
    kv_here = lax.all_to_all(kv, HEAD, 0, 0, tiled=True).reshape(SEQ_ROWS, 2 * HD)

    q = jnp.transpose(q_rows.reshape(ROWS, GROUPS, SLOTS * HD), (1, 0, 2))
    q_here = lax.all_to_all(q, HEAD, 0, 0, tiled=True).reshape(SEQ_ROWS, SLOTS * HD)

    kv_before = lax.ppermute(kv_here, SEQ, [(i, i + 1) for i in range(47)])

    chunks = jnp.transpose(kv_here.reshape(LB, 8, CH, 2, HD), (3, 1, 0, 2, 4))
    held = lax.all_to_all(chunks.reshape(SUB, LB, CH, HD), PART, 0, 0, tiled=True)
    owner = verts // LB
    z = (owner % 24) // 2
    spot = ((owner // 24) * 8 + (z % 4) * 2 + owner % 2) * LB + verts % LB
    mine = (z // 4 == za)[:, None, None]
    chosen = jnp.where(mine, held.reshape(SUB * LB, CH, HD)[spot], jnp.bfloat16(0))
    one = lax.ppermute(chosen, "za", [(0, 1), (1, 2), (2, 0)])
    two = lax.ppermute(chosen, "za", [(0, 2), (1, 0), (2, 1)])
    chosen = chosen + one + two
    spread = jnp.broadcast_to(chosen[None], (SUB, SLOTS * NV, CH, HD))
    vert = lax.all_to_all(spread, PART, 0, 0, tiled=True)

    meta = jnp.concatenate([seq_place[None].astype(jnp.int32), verts, offs])
    out = attention(meta, q_here, kv_here, kv_before, vert)
    back = lax.all_to_all(out.reshape(GROUPS, ROWS, SLOTS * HD), HEAD, 0, 0, tiled=True)
    return place_slots(group_assign, back)


def solution(mesh):
    fine = Mesh(mesh.devices.reshape(2, 3, 4, 2, 2, 8), ALL)
    rows = P(ALL, None)
    return jax.shard_map(
        per_device,
        mesh=fine,
        in_specs=(rows, rows, rows, P(), P(), P()),
        out_specs=rows,
        check_vma=False,
    )
```

```python
import math

import jax
import jax.numpy as jnp
from jax import lax
from jax.experimental import pallas as pl
from jax.experimental.pallas import tpu as pltpu
from jax.sharding import Mesh, PartitionSpec as P


QUERY_HEADS = 64
KEY_VALUE_HEADS = 8
HD = 128
BT = 128
NV = 4
NS = 3
GROUPS = 16
CORES = 2
SLOTS = QUERY_HEADS // GROUPS // CORES
ROWS = 40
SEQ_ROWS = 640
LB = SEQ_ROWS // BT
TOKENS = CORES * SEQ_ROWS
CHIP_WIDE = CORES * SLOTS * HD
WIDE = CHIP_WIDE + 2 * HD
CH = 16
SUB = 16
ALL = ("xl", "za", "zb", "c", "xh", "y")
HEAD = ("xh", "y")
SPLIT = ("c", "xh", "y")
PART = ("xl", "zb", "c")
SCALE = 1.0 / math.sqrt(HD)
NEG = float("-inf")


def attend(meta, here_ref, other_ref, prev_ref, vert_ref, o_ref, qs, win, vk, vv, kc, vc):
    first_block = meta[0]
    core = meta[1]
    wide = SLOTS * HD
    my_lanes = pl.ds(pl.multiple_of(core * wide, wide), wide)
    kv_lanes = slice(CORES * wide, CORES * wide + 2 * HD)
    mine = pl.multiple_of(core * SEQ_ROWS, SEQ_ROWS)
    theirs = pl.multiple_of((1 - core) * SEQ_ROWS, SEQ_ROWS)
    win[0:SEQ_ROWS, :] = prev_ref[...]
    win[pl.ds(SEQ_ROWS + mine, SEQ_ROWS), :] = here_ref[:, kv_lanes]
    win[pl.ds(SEQ_ROWS + theirs, SEQ_ROWS), :] = other_ref[:, kv_lanes]
    qs[pl.ds(mine, SEQ_ROWS), :] = here_ref[:, my_lanes]
    qs[pl.ds(theirs, SEQ_ROWS), :] = other_ref[:, my_lanes]
    causal = lax.broadcasted_iota(jnp.int32, (BT, BT), 0) >= lax.broadcasted_iota(
        jnp.int32, (BT, BT), 1
    )
    for j in range(SLOTS * NV):
        h, n = divmod(j, NV)
        vk[h, n * BT : (n + 1) * BT, :] = vert_ref[0:8, j].reshape(BT, HD)
        vv[h, n * BT : (n + 1) * BT, :] = vert_ref[8:16, j].reshape(BT, HD)

    def unit(step, carry):
        h = step // CORES
        half = step % CORES
        lane = pl.ds(pl.multiple_of(h * HD, HD), HD)
        offs = [meta[2 + SLOTS * NV + h * NS + n] for n in range(NS)]
        verts = [meta[2 + h * NV + n] for n in range(NV)]
        for i in range(LB):
            local = half * LB + i
            block = first_block + local
            good = []
            for n in range(NS):
                at = pl.ds(pl.multiple_of((LB + local - offs[n]) * BT, BT), BT)
                rows = slice(n * BT, (n + 1) * BT)
                kc[i, rows, :] = win[at, 0:HD]
                vc[i, rows, :] = win[at, HD : 2 * HD]
                good.append(block - offs[n] >= 0)
            for n in range(NV):
                ok = verts[n] <= block
                for o in offs:
                    ok = ok & (block - verts[n] != o)
                for e in range(n):
                    ok = ok & (verts[n] != verts[e])
                good.append(ok)
            rows = pl.ds(pl.multiple_of(local * BT, BT), BT)
            q = qs[rows, lane]
            dims = (((1,), (1,)), ((), ()))
            near = lax.dot_general(q, kc[i], dims, preferred_element_type=jnp.float32) * SCALE
            far = lax.dot_general(q, vk[h], dims, preferred_element_type=jnp.float32) * SCALE
            parts = [jnp.where(causal, near[:, 0:BT], NEG)]
            for n in range(1, NS):
                parts.append(near[:, n * BT : (n + 1) * BT] + jnp.where(good[n], 0.0, NEG))
            for n in range(NV):
                parts.append(far[:, n * BT : (n + 1) * BT] + jnp.where(good[NS + n], 0.0, NEG))
            top = parts[0]
            for x in parts[1:]:
                top = jnp.maximum(top, x)
            top = jnp.max(top, axis=1, keepdims=True)
            ws = [jnp.exp(x - top) for x in parts]
            total = ws[0]
            for x in ws[1:]:
                total = total + x
            total = jnp.sum(total, axis=1, keepdims=True)
            ws = [x.astype(jnp.bfloat16) for x in ws]
            acc = jnp.dot(
                jnp.concatenate(ws[:NS], axis=1), vc[i], preferred_element_type=jnp.float32
            ) + jnp.dot(jnp.concatenate(ws[NS:], axis=1), vv[h], preferred_element_type=jnp.float32)
            o_ref[rows, lane] = (acc / total).astype(jnp.bfloat16)
        return carry

    lax.fori_loop(0, SLOTS * CORES, unit, 0)


def attention(meta, here, other, prev, vert):
    vm = pl.BlockSpec(memory_space=pltpu.VMEM)
    return pl.pallas_call(
        attend,
        out_shape=jax.ShapeDtypeStruct((TOKENS, SLOTS * HD), jnp.bfloat16),
        in_specs=[pl.BlockSpec(memory_space=pltpu.SMEM), vm, vm, vm, vm],
        out_specs=vm,
        scratch_shapes=[
            pltpu.VMEM((TOKENS, SLOTS * HD), jnp.bfloat16),
            pltpu.VMEM((TOKENS + SEQ_ROWS, 2 * HD), jnp.bfloat16),
            pltpu.VMEM((SLOTS, NV * BT, HD), jnp.bfloat16),
            pltpu.VMEM((SLOTS, NV * BT, HD), jnp.bfloat16),
            pltpu.VMEM((LB, NS * BT, HD), jnp.bfloat16),
            pltpu.VMEM((LB, NS * BT, HD), jnp.bfloat16),
        ],
        name="attend",
    )(meta, here, other, prev, vert)


def lay_out(q_ref, k_ref, v_ref, o_ref):
    for g in range(GROUPS):
        m = g // (GROUPS // KEY_VALUE_HEADS)
        o_ref[g, :, 0:CHIP_WIDE] = q_ref[:, g * CHIP_WIDE : (g + 1) * CHIP_WIDE]
        o_ref[g, :, CHIP_WIDE : CHIP_WIDE + HD] = k_ref[:, m * HD : (m + 1) * HD]
        o_ref[g, :, CHIP_WIDE + HD : WIDE] = v_ref[:, m * HD : (m + 1) * HD]


def pack(q, k, v):
    vm = pl.BlockSpec(memory_space=pltpu.VMEM)
    return pl.pallas_call(
        lay_out,
        out_shape=jax.ShapeDtypeStruct((GROUPS, ROWS, WIDE), jnp.bfloat16),
        in_specs=[vm, vm, vm],
        out_specs=vm,
        name="lay_out",
    )(q, k, v)


def to_slots(assign, x_ref, o_ref):
    for k in range(QUERY_HEADS):
        a = assign[k]
        source = (a // SLOTS % CORES) * GROUPS + a // (SLOTS * CORES)
        lane = pl.ds(pl.multiple_of((a % SLOTS) * HD, HD), HD)
        o_ref[:, k * HD : (k + 1) * HD] = x_ref[source, :, lane]


def place_slots(assign, x):
    vm = pl.BlockSpec(memory_space=pltpu.VMEM)
    return pl.pallas_call(
        to_slots,
        out_shape=jax.ShapeDtypeStruct((ROWS, QUERY_HEADS * HD), jnp.bfloat16),
        in_specs=[pl.BlockSpec(memory_space=pltpu.SMEM), vm],
        out_specs=vm,
        name="to_slots",
    )(assign, x)


def per_device(q_rows, k_rows, v_rows, group_assign, vertical_blocks, slash_offsets):
    group = lax.axis_index(HEAD)
    core = lax.axis_index("c")
    chip = lax.axis_index(("xl", "za", "zb"))
    za = lax.axis_index("za")
    chip_heads = SLOTS * CORES
    verts = lax.dynamic_slice_in_dim(vertical_blocks, group * chip_heads, chip_heads).reshape(-1)
    my_head = group * chip_heads + core * SLOTS
    my_verts = lax.dynamic_slice_in_dim(vertical_blocks, my_head, SLOTS).reshape(-1)
    my_offs = lax.dynamic_slice_in_dim(slash_offsets, my_head, SLOTS).reshape(-1)

    sent = pack(q_rows, k_rows, v_rows)
    here = lax.all_to_all(sent, HEAD, 0, 0, tiled=True).reshape(SEQ_ROWS, WIDE)
    kv_here = here[:, CHIP_WIDE:]

    chunks = jnp.transpose(kv_here.reshape(LB, 8, CH, 2, HD), (3, 1, 0, 2, 4))
    held = lax.all_to_all(chunks.reshape(SUB, LB, CH, HD), PART, 0, 0, tiled=True)

    owner = verts // LB
    z = (owner % 24) // 2
    spot = ((owner // 24) * 8 + (z % 4) * 2 + owner % 2) * LB + verts % LB
    mine = (z // 4 == za)[:, None, None]
    chosen = jnp.where(mine, held.reshape(SUB * LB, CH, HD)[spot], jnp.bfloat16(0))
    slots = SLOTS * NV
    chosen = jnp.broadcast_to(
        chosen.reshape(1, CORES, slots, CH, HD), (3, CORES, slots, CH, HD)
    ).reshape(3 * CORES, slots, CH, HD)
    joined = lax.all_to_all(chosen, ("za", "c"), 0, 0, tiled=True)
    joined = joined.reshape(3, CORES, slots, CH, HD)
    joined = joined[0] + joined[1] + joined[2]
    spread = jnp.broadcast_to(joined[None], (8, CORES, slots, CH, HD))
    vert = lax.all_to_all(spread, ("xl", "zb"), 0, 0, tiled=True)

    other = lax.ppermute(here, "c", [(0, 1), (1, 0)])
    gated, _ = lax.optimization_barrier((other[:, CHIP_WIDE:], held))
    last = jnp.where(core == 1, kv_here, gated)
    kv_before = lax.ppermute(last, ("xl", "za", "zb"), [(i, i + 1) for i in range(23)])

    meta = jnp.concatenate(
        [jnp.stack([chip * CORES * LB, core]).astype(jnp.int32), my_verts, my_offs]
    )
    out = attention(meta, here, other, kv_before, vert.reshape(SUB, slots, CH, HD))
    back = lax.all_to_all(
        out.reshape(CORES * GROUPS, ROWS, SLOTS * HD), SPLIT, 0, 0, tiled=True
    )
    return place_slots(group_assign, back)


def solution(mesh):
    fine = Mesh(mesh.devices.reshape(2, 3, 4, 2, 2, 8), ALL)
    rows = P(ALL, None)
    return jax.shard_map(
        per_device,
        mesh=fine,
        in_specs=(rows, rows, rows, P(), P(), P()),
        out_specs=rows,
        check_vma=False,
    )
```

```python
import math

import jax
import jax.numpy as jnp
from jax import lax
from jax.experimental import pallas as pl
from jax.experimental.pallas import tpu as pltpu
from jax.sharding import Mesh, PartitionSpec as P


QUERY_HEADS = 64
KEY_VALUE_HEADS = 8
HD = 128
BT = 128
NV = 4
NS = 3
GROUPS = 16
CORES = 2
SLOTS = QUERY_HEADS // GROUPS // CORES
ROWS = 40
SEQ_ROWS = 640
LB = SEQ_ROWS // BT
TOKENS = CORES * SEQ_ROWS
CHIP_WIDE = CORES * SLOTS * HD
WIDE = CHIP_WIDE + 2 * HD
CHIP_SLOTS = CORES * SLOTS * NV
CH = 16
SUB = 16
ALL = ("xl", "za", "zb", "c", "xh", "y")
HEAD = ("xh", "y")
SPLIT = ("c", "xh", "y")
PART = ("xl", "zb", "c")
SCALE = 1.0 / math.sqrt(HD)
NEG = float("-inf")
SMALL = 4 * 1024 * 1024
PAIR = 2
LARGE = 12 * 1024 * 1024


LOG2E_SCALE = SCALE * math.log2(math.e)
DIMS = (((1,), (1,)), ((), ()))


def in_vmem(x):
    return pltpu.with_memory_space_constraint(x, pltpu.VMEM)


def in_hbm(x):
    return pltpu.with_memory_space_constraint(x, pltpu.HBM)


def near_part(meta, here_ref, other_ref, prev_ref, acc_ref, stat_ref, q_ref, win, kc, vc):
    first_block = meta[0]
    core = meta[1]
    wide = SLOTS * HD
    my_lanes = pl.ds(pl.multiple_of(core * wide, wide), wide)
    kv_lanes = slice(CORES * wide, CORES * wide + 2 * HD)
    mine = pl.multiple_of(core * SEQ_ROWS, SEQ_ROWS)
    theirs = pl.multiple_of((1 - core) * SEQ_ROWS, SEQ_ROWS)
    win[0:SEQ_ROWS, :] = prev_ref[...]
    win[pl.ds(SEQ_ROWS + mine, SEQ_ROWS), :] = here_ref[:, kv_lanes]
    win[pl.ds(SEQ_ROWS + theirs, SEQ_ROWS), :] = other_ref[:, kv_lanes]
    q_ref[pl.ds(mine, SEQ_ROWS), :] = here_ref[:, my_lanes]
    q_ref[pl.ds(theirs, SEQ_ROWS), :] = other_ref[:, my_lanes]
    causal = lax.broadcasted_iota(jnp.int32, (BT, BT), 0) >= lax.broadcasted_iota(
        jnp.int32, (BT, BT), 1
    )

    def unit(step, carry):
        for i in range(PAIR * SLOTS):
            h = i % SLOTS
            local = step * PAIR + i // SLOTS
            lane = slice(h * HD, (h + 1) * HD)
            offs = [meta[2 + SLOTS * NV + h * NS + n] for n in range(NS)]
            good = []
            for n in range(NS):
                at = pl.ds(pl.multiple_of((LB + local - offs[n]) * BT, BT), BT)
                rows = slice(n * BT, (n + 1) * BT)
                kc[i, rows, :] = win[at, 0:HD]
                vc[i, rows, :] = win[at, HD : 2 * HD]
                good.append(first_block + local - offs[n] >= 0)
            rows = pl.ds(pl.multiple_of(local * BT, BT), BT)
            s = lax.dot_general(q_ref[rows, lane], kc[i], DIMS, preferred_element_type=jnp.float32)
            parts = [jnp.where(causal, s[:, 0:BT], NEG)]
            for n in range(1, NS):
                parts.append(s[:, n * BT : (n + 1) * BT] + jnp.where(good[n], 0.0, NEG))
            top = jnp.maximum(jnp.maximum(parts[0], parts[1]), parts[2])
            top = jnp.max(top, axis=1, keepdims=True)
            ws = [jnp.exp2((x - top) * LOG2E_SCALE) for x in parts]
            total = jnp.sum(ws[0] + ws[1] + ws[2], axis=1, keepdims=True)
            w = jnp.concatenate([x.astype(jnp.bfloat16) for x in ws], axis=1)
            acc_ref[rows, lane] = jnp.dot(w, vc[i], preferred_element_type=jnp.float32)
            stat_ref[rows, 2 * h : 2 * h + 1] = top
            stat_ref[rows, 2 * h + 1 : 2 * h + 2] = total
        return carry

    lax.fori_loop(0, TOKENS // BT // PAIR, unit, 0)


def near(meta, here, other, prev):
    vm = pl.BlockSpec(memory_space=pltpu.VMEM)
    return pl.pallas_call(
        near_part,
        out_shape=(
            jax.ShapeDtypeStruct((TOKENS, SLOTS * HD), jnp.float32),
            pltpu.VMEM((TOKENS, HD), jnp.float32),
            pltpu.VMEM((TOKENS, SLOTS * HD), jnp.bfloat16),
        ),
        in_specs=[pl.BlockSpec(memory_space=pltpu.SMEM), vm, vm, vm],
        out_specs=(vm, vm, vm),
        scratch_shapes=[
            pltpu.VMEM((TOKENS + SEQ_ROWS, 2 * HD), jnp.bfloat16),
            pltpu.VMEM((PAIR * SLOTS, NS * BT, HD), jnp.bfloat16),
            pltpu.VMEM((PAIR * SLOTS, NS * BT, HD), jnp.bfloat16),
        ],
        name="near",
        compiler_params=pltpu.CompilerParams(vmem_limit_bytes=LARGE),
    )(meta, in_vmem(here), in_vmem(other), in_vmem(prev))


def far_part(meta, q_ref, acc_hbm, stat_ref, vert_ref, o_ref, acc_ref, vk, vv, sems):
    first_block = meta[0]
    steps = TOKENS // BT // PAIR

    def fetch(step):
        rows = pl.ds(pl.multiple_of(step * PAIR * BT, PAIR * BT), PAIR * BT)
        return pltpu.make_async_copy(acc_hbm.at[rows], acc_ref.at[rows], sems.at[step])

    for step in range(steps):
        fetch(step).start()
    for j in range(SLOTS * NV):
        h, n = divmod(j, NV)
        vk[h, n * BT : (n + 1) * BT, :] = vert_ref[0:8, j].reshape(BT, HD)
        vv[h, n * BT : (n + 1) * BT, :] = vert_ref[8:16, j].reshape(BT, HD)

    def unit(step, carry):
        fetch(step).wait()
        for i in range(PAIR * SLOTS):
            h = i % SLOTS
            local = step * PAIR + i // SLOTS
            lane = slice(h * HD, (h + 1) * HD)
            offs = [meta[2 + SLOTS * NV + h * NS + n] for n in range(NS)]
            verts = [meta[2 + h * NV + n] for n in range(NV)]
            block = first_block + local
            rows = pl.ds(pl.multiple_of(local * BT, BT), BT)
            s = lax.dot_general(q_ref[rows, lane], vk[h], DIMS, preferred_element_type=jnp.float32)
            parts = []
            for n in range(NV):
                ok = verts[n] <= block
                for o in offs:
                    ok = ok & (block - verts[n] != o)
                for e in range(n):
                    ok = ok & (verts[n] != verts[e])
                parts.append(s[:, n * BT : (n + 1) * BT] + jnp.where(ok, 0.0, NEG))
            old = stat_ref[rows, 2 * h : 2 * h + 1]
            top = jnp.maximum(
                jnp.maximum(parts[0], parts[1]), jnp.maximum(parts[2], parts[3])
            )
            top = jnp.maximum(jnp.max(top, axis=1, keepdims=True), old)
            keep = jnp.exp2((old - top) * LOG2E_SCALE)
            ws = [jnp.exp2((x - top) * LOG2E_SCALE) for x in parts]
            total = jnp.sum((ws[0] + ws[1]) + (ws[2] + ws[3]), axis=1, keepdims=True)
            total = total + stat_ref[rows, 2 * h + 1 : 2 * h + 2] * keep
            w = jnp.concatenate([x.astype(jnp.bfloat16) for x in ws], axis=1)
            acc = acc_ref[rows, lane] * keep + jnp.dot(
                w, vv[h], preferred_element_type=jnp.float32
            )
            o_ref[rows, lane] = (acc / total).astype(jnp.bfloat16)
        return carry

    lax.fori_loop(0, steps, unit, 0)


def far(meta, q, acc, stat, vert):
    vm = pl.BlockSpec(memory_space=pltpu.VMEM)
    return pl.pallas_call(
        far_part,
        out_shape=pltpu.VMEM((TOKENS, SLOTS * HD), jnp.bfloat16),
        in_specs=[
            pl.BlockSpec(memory_space=pltpu.SMEM),
            vm,
            pl.BlockSpec(memory_space=pltpu.HBM),
            vm,
            vm,
        ],
        out_specs=vm,
        scratch_shapes=[
            pltpu.VMEM((TOKENS, SLOTS * HD), jnp.float32),
            pltpu.VMEM((SLOTS, NV * BT, HD), jnp.bfloat16),
            pltpu.VMEM((SLOTS, NV * BT, HD), jnp.bfloat16),
            pltpu.SemaphoreType.DMA((TOKENS // BT // PAIR,)),
        ],
        name="far",
        compiler_params=pltpu.CompilerParams(vmem_limit_bytes=LARGE),
    )(meta, in_vmem(q), in_hbm(acc), in_vmem(stat), in_vmem(vert))


def cut(here_ref, o_ref):
    for j in range(LB):
        for r in range(BT // CH):
            rows = slice(j * BT + r * CH, j * BT + (r + 1) * CH)
            o_ref[r, j] = here_ref[rows, CHIP_WIDE : CHIP_WIDE + HD]
            o_ref[BT // CH + r, j] = here_ref[rows, CHIP_WIDE + HD : WIDE]


def in_chunks(here):
    vm = pl.BlockSpec(memory_space=pltpu.VMEM)
    return pl.pallas_call(
        cut,
        out_shape=pltpu.VMEM((SUB, LB, CH, HD), jnp.bfloat16),
        in_specs=[vm],
        out_specs=vm,
        name="cut",
        compiler_params=pltpu.CompilerParams(vmem_limit_bytes=SMALL),
    )(in_vmem(here))


def newest(core, here_ref, other_ref, o_ref):
    @pl.when(core[0] == 1)
    def _():
        o_ref[...] = here_ref[:, CHIP_WIDE:WIDE]

    @pl.when(core[0] != 1)
    def _():
        o_ref[...] = other_ref[:, CHIP_WIDE:WIDE]


def last_window(core, here, other):
    vm = pl.BlockSpec(memory_space=pltpu.VMEM)
    return pl.pallas_call(
        newest,
        out_shape=pltpu.VMEM((SEQ_ROWS, 2 * HD), jnp.bfloat16),
        in_specs=[pl.BlockSpec(memory_space=pltpu.SMEM), vm, vm],
        out_specs=vm,
        name="newest",
        compiler_params=pltpu.CompilerParams(vmem_limit_bytes=SMALL),
    )(core, in_vmem(here), in_vmem(other))


def choose(spots, held_ref, o_ref):
    for c in range(CORES):
        for j in range(SLOTS * NV):
            at = c * SLOTS * NV + j
            x = held_ref[spots[at]] * jnp.where(spots[CHIP_SLOTS + at] == 1, 1.0, 0.0).astype(
                jnp.bfloat16
            )
            for part in range(3):
                o_ref[part * CORES + c, j] = x


def chosen_chunks(spots, held):
    vm = pl.BlockSpec(memory_space=pltpu.VMEM)
    return pl.pallas_call(
        choose,
        out_shape=pltpu.VMEM((3 * CORES, SLOTS * NV, CH, HD), jnp.bfloat16),
        in_specs=[pl.BlockSpec(memory_space=pltpu.SMEM), vm],
        out_specs=vm,
        name="choose",
        compiler_params=pltpu.CompilerParams(vmem_limit_bytes=SMALL),
    )(spots, in_vmem(held))


def add_up(x_ref, o_ref):
    for c in range(CORES):
        total = x_ref[c] + x_ref[CORES + c] + x_ref[2 * CORES + c]
        for part in range(8):
            o_ref[part, c] = total


def copies_of_sum(x):
    vm = pl.BlockSpec(memory_space=pltpu.VMEM)
    return pl.pallas_call(
        add_up,
        out_shape=jax.ShapeDtypeStruct((8, CORES, SLOTS * NV, CH, HD), jnp.bfloat16),
        in_specs=[vm],
        out_specs=vm,
        name="add_up",
        compiler_params=pltpu.CompilerParams(vmem_limit_bytes=SMALL),
    )(in_vmem(x))


def lay_out(q_ref, k_ref, v_ref, o_ref, sems):
    copies = []
    for g in range(GROUPS):
        m = g // (GROUPS // KEY_VALUE_HEADS) * HD
        for n, (ref, start, at, size) in enumerate(
            (
                (q_ref, g * CHIP_WIDE, 0, CHIP_WIDE),
                (k_ref, m, CHIP_WIDE, HD),
                (v_ref, m, CHIP_WIDE + HD, HD),
            )
        ):
            copies.append(
                pltpu.make_async_copy(
                    ref.at[:, pl.ds(start, size)], o_ref.at[g, :, pl.ds(at, size)], sems.at[n, g]
                )
            )
    for copy in copies:
        copy.start()
    for copy in copies:
        copy.wait()


def pack(q, k, v):
    anywhere = pl.BlockSpec(memory_space=pltpu.HBM)
    return pl.pallas_call(
        lay_out,
        out_shape=pltpu.VMEM((GROUPS, ROWS, WIDE), jnp.bfloat16),
        in_specs=[anywhere] * 3,
        out_specs=pl.BlockSpec(memory_space=pltpu.VMEM),
        scratch_shapes=[pltpu.SemaphoreType.DMA((3, GROUPS))],
        name="lay_out",
        compiler_params=pltpu.CompilerParams(vmem_limit_bytes=SMALL),
    )(in_hbm(q), in_hbm(k), in_hbm(v))


def to_slots(assign, x_ref, o_ref, sems):
    copies = []
    for k in range(QUERY_HEADS):
        a = assign[k]
        source = (a >> 1 & 1) * GROUPS + (a >> 2)
        lane = pl.ds(pl.multiple_of((a & 1) * HD, HD), HD)
        copies.append(
            pltpu.make_async_copy(
                x_ref.at[source, :, lane], o_ref.at[:, pl.ds(k * HD, HD)], sems.at[k]
            )
        )
        copies[-1].start()
    for copy in copies:
        copy.wait()


def place_slots(assign, x):
    return pl.pallas_call(
        to_slots,
        out_shape=jax.ShapeDtypeStruct((ROWS, QUERY_HEADS * HD), jnp.bfloat16),
        in_specs=[
            pl.BlockSpec(memory_space=pltpu.SMEM),
            pl.BlockSpec(memory_space=pltpu.VMEM),
        ],
        out_specs=pl.BlockSpec(memory_space=pl.ANY),
        scratch_shapes=[pltpu.SemaphoreType.DMA((QUERY_HEADS,))],
        name="to_slots",
        compiler_params=pltpu.CompilerParams(vmem_limit_bytes=SMALL),
    )(assign, in_vmem(x))


def per_device(q_rows, k_rows, v_rows, group_assign, vertical_blocks, slash_offsets):
    group = lax.axis_index(HEAD)
    core = lax.axis_index("c")
    chip = lax.axis_index(("xl", "za", "zb"))
    za = lax.axis_index("za")
    chip_heads = SLOTS * CORES
    verts = lax.dynamic_slice_in_dim(vertical_blocks, group * chip_heads, chip_heads).reshape(-1)
    my_head = group * chip_heads + core * SLOTS
    my_verts = lax.dynamic_slice_in_dim(vertical_blocks, my_head, SLOTS).reshape(-1)
    my_offs = lax.dynamic_slice_in_dim(slash_offsets, my_head, SLOTS).reshape(-1)

    sent = pack(q_rows, k_rows, v_rows)
    here = lax.all_to_all(sent, HEAD, 0, 0, tiled=True).reshape(SEQ_ROWS, WIDE)
    held = lax.all_to_all(in_chunks(here), PART, 0, 0, tiled=True)

    other = lax.ppermute(here, "c", [(0, 1), (1, 0)])
    last = last_window(core.reshape(1), here, other)
    kv_before = lax.ppermute(last, ("xl", "za", "zb"), [(i, i + 1) for i in range(23)])
    meta = jnp.concatenate(
        [jnp.stack([chip * CORES * LB, core]).astype(jnp.int32), my_verts, my_offs]
    )

    owner = verts // LB
    z = (owner % 24) // 2
    spot = ((owner // 24) * 8 + (z % 4) * 2 + owner % 2) * LB + verts % LB
    spots = jnp.concatenate([spot, (z // 4 == za).astype(jnp.int32)])
    chosen = chosen_chunks(spots, held.reshape(SUB * LB, CH, HD))
    joined = lax.all_to_all(chosen, ("za", "c"), 0, 0, tiled=True)
    spread = copies_of_sum(joined)
    vert = lax.all_to_all(spread, ("xl", "zb"), 0, 0, tiled=True)
    slots = SLOTS * NV
    acc, stat, q_here = near(meta, here, other, kv_before)
    out = far(meta, q_here, acc, stat, vert.reshape(SUB, slots, CH, HD))
    back = lax.all_to_all(
        out.reshape(CORES * GROUPS, ROWS, SLOTS * HD), SPLIT, 0, 0, tiled=True
    )
    return place_slots(group_assign, back)


def solution(mesh):
    fine = Mesh(mesh.devices.reshape(2, 3, 4, 2, 2, 8), ALL)
    rows = P(ALL, None)
    return jax.shard_map(
        per_device,
        mesh=fine,
        in_specs=(rows, rows, rows, P(), P(), P()),
        out_specs=rows,
        check_vma=False,
    )
```

```python
import math

import jax
import jax.numpy as jnp
from jax import lax
from jax.experimental import pallas as pl
from jax.experimental.pallas import tpu as pltpu
from jax.sharding import Mesh, PartitionSpec as P


QUERY_HEADS = 64
HD = 128
BT = 128
NV = 4
NS = 3
GROUPS = 16
CORES = 2
SLOTS = QUERY_HEADS // GROUPS // CORES
ROWS = 40
SEQ_ROWS = 640
LB = SEQ_ROWS // BT
TOKENS = CORES * SEQ_ROWS
CHIP_WIDE = CORES * SLOTS * HD
WIDE = CHIP_WIDE + HD
MINE = SLOTS * NV
PAIR_SLOTS = 2 * CORES * MINE
CH = 8
SUB = 16
ALL = ("xl", "za", "zb", "c", "xh", "ya", "yb")
HEAD = ("xh", "ya", "yb")
SPLIT = ("c", "xh", "ya", "yb")
PART = ("xl", "zb", "c")
SCALE = 1.0 / math.sqrt(HD)
NEG = float("-inf")
SMALL = 4 * 1024 * 1024
PAIR = 5
LARGE = 12 * 1024 * 1024


LOG2E_SCALE = SCALE * math.log2(math.e)
DIMS = (((1,), (1,)), ((), ()))


def in_vmem(x):
    return pltpu.with_memory_space_constraint(x, pltpu.VMEM)


def in_hbm(x):
    return pltpu.with_memory_space_constraint(x, pltpu.HBM)


def both_kinds(meta, here_ref, other_ref, pair_ref, diag_ref):
    own = pl.ds(pl.multiple_of(meta[2] * HD, HD), HD)
    rest = pl.ds(pl.multiple_of((1 - meta[2]) * HD, HD), HD)
    x = slice(CHIP_WIDE, WIDE)
    return ((own, here_ref.at[:, x], other_ref.at[:, x]), (rest, pair_ref, diag_ref))


def near_part(
    meta,
    here_ref,
    other_ref,
    pair_ref,
    diag_ref,
    prev_ref,
    acc_ref,
    top_ref,
    q_ref,
    win,
    kc,
    vc,
):
    first_block = meta[0]
    core = meta[1]
    wide = SLOTS * HD
    my_lanes = pl.ds(pl.multiple_of(core * wide, wide), wide)
    mine = pl.multiple_of(core * SEQ_ROWS, SEQ_ROWS)
    theirs = pl.multiple_of((1 - core) * SEQ_ROWS, SEQ_ROWS)
    win[0:SEQ_ROWS, :] = prev_ref[...]
    for lanes, inner, outer in both_kinds(meta, here_ref, other_ref, pair_ref, diag_ref):
        win[pl.ds(SEQ_ROWS + mine, SEQ_ROWS), lanes] = inner[...]
        win[pl.ds(SEQ_ROWS + theirs, SEQ_ROWS), lanes] = outer[...]
    q_ref[pl.ds(mine, SEQ_ROWS), :] = here_ref[:, my_lanes]
    q_ref[pl.ds(theirs, SEQ_ROWS), :] = other_ref[:, my_lanes]
    for i in range(PAIR * SLOTS):
        vc[i, :, HD : 2 * HD] = jnp.ones((NS * BT, HD), jnp.bfloat16)
    causal = lax.broadcasted_iota(jnp.int32, (BT, BT), 0) >= lax.broadcasted_iota(
        jnp.int32, (BT, BT), 1
    )

    def unit(step, carry):
        for i in range(PAIR * SLOTS):
            h = i % SLOTS
            local = step * PAIR + i // SLOTS
            offs = [meta[3 + MINE + h * NS + n] for n in range(NS)]
            good = []
            for n in range(NS):
                at = pl.ds(pl.multiple_of((LB + local - offs[n]) * BT, BT), BT)
                rows = slice(n * BT, (n + 1) * BT)
                kc[i, rows, :] = win[at, 0:HD]
                vc[i, rows, 0:HD] = win[at, HD : 2 * HD]
                good.append(first_block + local - offs[n] >= 0)
            rows = pl.ds(pl.multiple_of(local * BT, BT), BT)
            q = q_ref[rows, h * HD : (h + 1) * HD]
            s = lax.dot_general(q, kc[i], DIMS, preferred_element_type=jnp.float32)
            parts = [jnp.where(causal, s[:, 0:BT], NEG)]
            for n in range(1, NS):
                parts.append(s[:, n * BT : (n + 1) * BT] + jnp.where(good[n], 0.0, NEG))
            top = jnp.maximum(jnp.maximum(parts[0], parts[1]), parts[2])
            top = jnp.broadcast_to(jnp.max(top, axis=1, keepdims=True), (BT, HD))
            w = jnp.concatenate(
                [jnp.exp2((x - top) * LOG2E_SCALE).astype(jnp.bfloat16) for x in parts], axis=1
            )
            acc_ref[rows, 2 * h * HD : 2 * (h + 1) * HD] = jnp.dot(
                w, vc[i], preferred_element_type=jnp.float32
            )
            top_ref[rows, h * HD : (h + 1) * HD] = top
        return carry

    lax.fori_loop(0, TOKENS // BT // PAIR, unit, 0)


def near(meta, here, other, pair, diag, prev):
    vm = pl.BlockSpec(memory_space=pltpu.VMEM)
    return pl.pallas_call(
        near_part,
        out_shape=(
            jax.ShapeDtypeStruct((TOKENS, 2 * SLOTS * HD), jnp.float32),
            jax.ShapeDtypeStruct((TOKENS, SLOTS * HD), jnp.float32),
            jax.ShapeDtypeStruct((TOKENS, SLOTS * HD), jnp.bfloat16),
        ),
        in_specs=[pl.BlockSpec(memory_space=pltpu.SMEM), vm, vm, vm, vm, vm],
        out_specs=(vm, vm, vm),
        scratch_shapes=[
            pltpu.VMEM((TOKENS + SEQ_ROWS, 2 * HD), jnp.bfloat16),
            pltpu.VMEM((PAIR * SLOTS, NS * BT, HD), jnp.bfloat16),
            pltpu.VMEM((PAIR * SLOTS, NS * BT, 2 * HD), jnp.bfloat16),
        ],
        name="near",
        compiler_params=pltpu.CompilerParams(vmem_limit_bytes=LARGE),
    )(meta, *(in_vmem(x) for x in (here, other, pair, diag, prev)))


def far_part(
    meta, q_hbm, acc_hbm, top_hbm, vert_ref, o_ref, q_ref, acc_ref, top_ref, vk, vv, sems
):
    first_block = meta[0]
    steps = TOKENS // BT // PAIR
    moves = ((q_hbm, q_ref), (top_hbm, top_ref), (acc_hbm, acc_ref))

    def fetch(step):
        rows = pl.ds(pl.multiple_of(step * PAIR * BT, PAIR * BT), PAIR * BT)
        return [
            pltpu.make_async_copy(source.at[rows], target.at[rows], sems.at[n, step])
            for n, (source, target) in enumerate(moves)
        ]

    for step in range(steps):
        for copy in fetch(step):
            copy.start()
    for h in range(SLOTS):
        vv[h, :, HD : 2 * HD] = jnp.ones((NV * BT, HD), jnp.bfloat16)
        for n in range(NV):
            rows = slice(n * BT, (n + 1) * BT)
            for kind, target in ((0, vk), (1, vv)):
                x = vert_ref[:, kind, h * NV + n].astype(jnp.float32).reshape(BT, HD)
                target[h, rows, 0:HD] = x.astype(jnp.bfloat16)

    def unit(step, carry):
        moving = fetch(step)
        moving[0].wait()
        moving[1].wait()
        later = []
        both = pl.ds(pl.multiple_of(step * PAIR * BT, PAIR * BT), PAIR * BT)
        for h in range(SLOTS):
            offs = [meta[3 + MINE + h * NS + n] for n in range(NS)]
            verts = [meta[3 + h * NV + n] for n in range(NV)]
            lane = slice(h * HD, (h + 1) * HD)
            s = lax.dot_general(q_ref[both, lane], vk[h], DIMS, preferred_element_type=jnp.float32)
            ws = []
            keeps = []
            for p in range(PAIR):
                local = step * PAIR + p
                block = first_block + local
                parts = []
                for n in range(NV):
                    ok = verts[n] <= block
                    for o in offs:
                        ok = ok & (block - verts[n] != o)
                    for e in range(n):
                        ok = ok & (verts[n] != verts[e])
                    x = s[p * BT : (p + 1) * BT, n * BT : (n + 1) * BT]
                    parts.append(x + jnp.where(ok, 0.0, NEG))
                rows = pl.ds(pl.multiple_of(local * BT, BT), BT)
                old = top_ref[rows, lane]
                top = jnp.maximum(
                    jnp.maximum(parts[0], parts[1]), jnp.maximum(parts[2], parts[3])
                )
                top = jnp.maximum(
                    jnp.broadcast_to(jnp.max(top, axis=1, keepdims=True), (BT, HD)), old
                )
                keeps.append(jnp.exp2((old - top) * LOG2E_SCALE))
                ws.append(
                    jnp.concatenate(
                        [jnp.exp2((x - top) * LOG2E_SCALE).astype(jnp.bfloat16) for x in parts],
                        axis=1,
                    )
                )
            gain = jnp.dot(
                jnp.concatenate(ws, axis=0), vv[h], preferred_element_type=jnp.float32
            )
            later.append((keeps, gain))
        moving[2].wait()
        for h, (keeps, gain) in enumerate(later):
            lane = slice(h * HD, (h + 1) * HD)
            for p in range(PAIR):
                rows = pl.ds(pl.multiple_of((step * PAIR + p) * BT, BT), BT)
                here = slice(p * BT, (p + 1) * BT)
                acc = acc_ref[rows, 2 * h * HD : (2 * h + 1) * HD] * keeps[p] + gain[here, 0:HD]
                total = (
                    acc_ref[rows, (2 * h + 1) * HD : (2 * h + 2) * HD] * keeps[p]
                    + gain[here, HD : 2 * HD]
                )
                o_ref[rows, lane] = (acc / total).astype(jnp.bfloat16)
        return carry

    lax.fori_loop(0, steps, unit, 0)


def far(meta, q, acc, top, vert):
    vm = pl.BlockSpec(memory_space=pltpu.VMEM)
    hbm = pl.BlockSpec(memory_space=pltpu.HBM)
    return pl.pallas_call(
        far_part,
        out_shape=pltpu.VMEM((TOKENS, SLOTS * HD), jnp.bfloat16),
        in_specs=[pl.BlockSpec(memory_space=pltpu.SMEM), hbm, hbm, hbm, vm],
        out_specs=vm,
        scratch_shapes=[
            pltpu.VMEM((TOKENS, SLOTS * HD), jnp.bfloat16),
            pltpu.VMEM((TOKENS, 2 * SLOTS * HD), jnp.float32),
            pltpu.VMEM((TOKENS, SLOTS * HD), jnp.float32),
            pltpu.VMEM((SLOTS, NV * BT, HD), jnp.bfloat16),
            pltpu.VMEM((SLOTS, NV * BT, 2 * HD), jnp.bfloat16),
            pltpu.SemaphoreType.DMA((3, TOKENS // BT // PAIR)),
        ],
        name="far",
        compiler_params=pltpu.CompilerParams(vmem_limit_bytes=LARGE),
    )(meta, in_hbm(q), in_hbm(acc), in_hbm(top), in_vmem(vert))


def cut(here_ref, o_ref, x_ref):
    x_ref[...] = here_ref[:, CHIP_WIDE:WIDE]
    for j in range(LB):
        x = here_ref[j * BT : (j + 1) * BT, CHIP_WIDE:WIDE].astype(jnp.float32)
        for r in range(SUB):
            o_ref[r, j] = x[r * CH : (r + 1) * CH].astype(jnp.bfloat16)


def in_chunks(here):
    vm = pl.BlockSpec(memory_space=pltpu.VMEM)
    return pl.pallas_call(
        cut,
        out_shape=(
            pltpu.VMEM((SUB, LB, CH, HD), jnp.bfloat16),
            pltpu.VMEM((SEQ_ROWS, HD), jnp.bfloat16),
        ),
        in_specs=[vm],
        out_specs=(vm, vm),
        name="cut",
        compiler_params=pltpu.CompilerParams(vmem_limit_bytes=SMALL),
    )(in_vmem(here))


def newest(meta, here_ref, other_ref, pair_ref, diag_ref, o_ref):
    for lanes, inner, outer in both_kinds(meta, here_ref, other_ref, pair_ref, diag_ref):

        @pl.when(meta[1] == 1)
        def _():
            o_ref[:, lanes] = inner[...]

        @pl.when(meta[1] != 1)
        def _():
            o_ref[:, lanes] = outer[...]


def last_window(meta, here, other, pair, diag):
    vm = pl.BlockSpec(memory_space=pltpu.VMEM)
    return pl.pallas_call(
        newest,
        out_shape=pltpu.VMEM((SEQ_ROWS, 2 * HD), jnp.bfloat16),
        in_specs=[pl.BlockSpec(memory_space=pltpu.SMEM), vm, vm, vm, vm],
        out_specs=vm,
        name="newest",
        compiler_params=pltpu.CompilerParams(vmem_limit_bytes=SMALL),
    )(meta, *(in_vmem(x) for x in (here, other, pair, diag)))


def choose(spots, held_ref, o_ref):
    for pair in range(2):
        for c in range(CORES):
            for j in range(MINE):
                at = (pair * CORES + c) * MINE + j
                mine = jnp.where(spots[PAIR_SLOTS + at] == 1, 1.0, 0.0).astype(jnp.bfloat16)
                x = held_ref[spots[at]] * mine
                for part in range(3):
                    o_ref[(part * CORES + c) * 2 + pair, j] = x


def chosen_chunks(spots, held):
    vm = pl.BlockSpec(memory_space=pltpu.VMEM)
    return pl.pallas_call(
        choose,
        out_shape=pltpu.VMEM((3 * CORES * 2, MINE, CH, HD), jnp.bfloat16),
        in_specs=[pl.BlockSpec(memory_space=pltpu.SMEM), vm],
        out_specs=vm,
        name="choose",
        compiler_params=pltpu.CompilerParams(vmem_limit_bytes=SMALL),
    )(spots, in_vmem(held))


def add_up(x_ref, o_ref):
    kinds = CORES * 2
    for c in range(kinds):
        total = x_ref[c] + x_ref[kinds + c] + x_ref[2 * kinds + c]
        for part in range(8):
            o_ref[part, c] = total


def copies_of_sum(x):
    vm = pl.BlockSpec(memory_space=pltpu.VMEM)
    return pl.pallas_call(
        add_up,
        out_shape=jax.ShapeDtypeStruct((8, CORES * 2, MINE, CH, HD), jnp.bfloat16),
        in_specs=[vm],
        out_specs=vm,
        name="add_up",
        compiler_params=pltpu.CompilerParams(vmem_limit_bytes=SMALL),
    )(in_vmem(x))


def lay_out(q_ref, k_ref, v_ref, o_ref, sems):
    copies = []
    for g in range(GROUPS):
        m = g // 2 * HD
        for n, (ref, start, at, size) in enumerate(
            (
                (q_ref, g * CHIP_WIDE, 0, CHIP_WIDE),
                (v_ref if g % 2 else k_ref, m, CHIP_WIDE, HD),
            )
        ):
            copies.append(
                pltpu.make_async_copy(
                    ref.at[:, pl.ds(start, size)], o_ref.at[g, :, pl.ds(at, size)], sems.at[n, g]
                )
            )
    for copy in copies:
        copy.start()
    for copy in copies:
        copy.wait()


def pack(q, k, v):
    anywhere = pl.BlockSpec(memory_space=pltpu.HBM)
    return pl.pallas_call(
        lay_out,
        out_shape=pltpu.VMEM((GROUPS, ROWS, WIDE), jnp.bfloat16),
        in_specs=[anywhere] * 3,
        out_specs=pl.BlockSpec(memory_space=pltpu.VMEM),
        scratch_shapes=[pltpu.SemaphoreType.DMA((2, GROUPS))],
        name="lay_out",
        compiler_params=pltpu.CompilerParams(vmem_limit_bytes=SMALL),
    )(in_hbm(q), in_hbm(k), in_hbm(v))


def to_slots(assign, x_ref, o_ref, sems):
    copies = []
    for k in range(QUERY_HEADS):
        a = assign[k]
        source = (a >> 1 & 1) * GROUPS + (a >> 2)
        lane = pl.ds(pl.multiple_of((a & 1) * HD, HD), HD)
        copies.append(
            pltpu.make_async_copy(
                x_ref.at[source, :, lane], o_ref.at[:, pl.ds(k * HD, HD)], sems.at[k]
            )
        )
        copies[-1].start()
    for copy in copies:
        copy.wait()


def place_slots(assign, x):
    return pl.pallas_call(
        to_slots,
        out_shape=jax.ShapeDtypeStruct((ROWS, QUERY_HEADS * HD), jnp.bfloat16),
        in_specs=[
            pl.BlockSpec(memory_space=pltpu.SMEM),
            pl.BlockSpec(memory_space=pltpu.VMEM),
        ],
        out_specs=pl.BlockSpec(memory_space=pl.ANY),
        scratch_shapes=[pltpu.SemaphoreType.DMA((QUERY_HEADS,))],
        name="to_slots",
        compiler_params=pltpu.CompilerParams(vmem_limit_bytes=SMALL),
    )(assign, in_vmem(x))


def per_device(q_rows, k_rows, v_rows, group_assign, vertical_blocks, slash_offsets):
    group = lax.axis_index(HEAD)
    core = lax.axis_index("c")
    odd = lax.axis_index("yb")
    chip = lax.axis_index(("xl", "za", "zb"))
    za = lax.axis_index("za")
    pair_heads = 2 * CORES * SLOTS
    verts = lax.dynamic_slice_in_dim(vertical_blocks, group // 2 * pair_heads, pair_heads)
    verts = verts.reshape(-1)
    my_head = (group * CORES + core) * SLOTS
    my_verts = lax.dynamic_slice_in_dim(vertical_blocks, my_head, SLOTS).reshape(-1)
    my_offs = lax.dynamic_slice_in_dim(slash_offsets, my_head, SLOTS).reshape(-1)
    place = jnp.stack([chip * CORES * LB, core, odd]).astype(jnp.int32)
    meta = jnp.concatenate([place, my_verts, my_offs])

    sent = pack(q_rows, k_rows, v_rows)
    here = lax.all_to_all(sent, HEAD, 0, 0, tiled=True).reshape(SEQ_ROWS, WIDE)
    chunks, x_here = in_chunks(here)
    held = lax.all_to_all(chunks, PART, 0, 0, tiled=True)

    other = lax.ppermute(here, "c", [(0, 1), (1, 0)])
    pair = lax.ppermute(x_here, "yb", [(0, 1), (1, 0)])
    diag = lax.ppermute(x_here, ("c", "yb"), [(0, 3), (1, 2), (2, 1), (3, 0)])
    last = last_window(place, here, other, pair, diag)
    kv_before = lax.ppermute(last, ("xl", "za", "zb"), [(i, i + 1) for i in range(23)])

    owner = verts // LB
    z = (owner % 24) // 2
    spot = ((owner // 24) * 8 + (z % 4) * 2 + owner % 2) * LB + verts % LB
    spots = jnp.concatenate([spot, (z // 4 == za).astype(jnp.int32)])
    chosen = chosen_chunks(spots, held.reshape(SUB * LB, CH, HD))
    joined = lax.all_to_all(chosen, ("za", "c", "yb"), 0, 0, tiled=True)
    spread = copies_of_sum(joined)
    vert = lax.all_to_all(spread, ("xl", "zb"), 0, 0, tiled=True)
    acc, top, q_here = near(meta, here, other, pair, diag, kv_before)
    out = far(meta, q_here, acc, top, vert.reshape(SUB, 2, MINE, CH, HD))
    back = lax.all_to_all(
        out.reshape(CORES * GROUPS, ROWS, SLOTS * HD), SPLIT, 0, 0, tiled=True
    )
    return place_slots(group_assign, back)


def solution(mesh):
    fine = Mesh(mesh.devices.reshape(2, 3, 4, 2, 2, 4, 2), ALL)
    rows = P(ALL, None)
    return jax.shard_map(
        per_device,
        mesh=fine,
        in_specs=(rows, rows, rows, P(), P(), P()),
        out_specs=rows,
        check_vma=False,
    )
```

```python
import math

import jax
import jax.numpy as jnp
from jax import lax
from jax.experimental import pallas as pl
from jax.experimental.pallas import tpu as pltpu
from jax.sharding import Mesh, PartitionSpec as P


QUERY_HEADS = 64
HD = 128
BT = 128
NV = 4
NS = 3
GROUPS = 16
CORES = 2
SLOTS = QUERY_HEADS // GROUPS // CORES
ROWS = 40
SEQ_ROWS = 640
LB = SEQ_ROWS // BT
TOKENS = CORES * SEQ_ROWS
CHIP_WIDE = CORES * SLOTS * HD
WIDE = CHIP_WIDE + HD
MINE = SLOTS * NV
PAIR_SLOTS = 2 * CORES * MINE
CH = 8
SUB = 16
ALL = ("xl", "za", "zb", "c", "xh", "ya", "yb")
HEAD = ("xh", "ya", "yb")
SPLIT = ("c", "xh", "ya", "yb")
PART = ("xl", "zb", "c")
SCALE = 1.0 / math.sqrt(HD)
NEG = float("-inf")
SMALL = 4 * 1024 * 1024
PAIR = 5
LARGE = 12 * 1024 * 1024


LOG2E_SCALE = SCALE * math.log2(math.e)
DIMS = (((1,), (1,)), ((), ()))


def in_vmem(x):
    return pltpu.with_memory_space_constraint(x, pltpu.VMEM)


def in_smem(x):
    return pltpu.with_memory_space_constraint(x, pltpu.SMEM)


def in_hbm(x):
    return pltpu.with_memory_space_constraint(x, pltpu.HBM)


def both_kinds(meta, here_ref, other_ref, pair_ref, diag_ref):
    own = pl.ds(pl.multiple_of(meta[2] * HD, HD), HD)
    rest = pl.ds(pl.multiple_of((1 - meta[2]) * HD, HD), HD)
    x = slice(CHIP_WIDE, WIDE)
    return ((own, here_ref.at[:, x], other_ref.at[:, x]), (rest, pair_ref, diag_ref))


def near_part(
    meta,
    here_ref,
    other_ref,
    pair_ref,
    diag_ref,
    prev_ref,
    acc_ref,
    top_ref,
    q_ref,
    win,
    kc,
    vc,
):
    first_block = meta[0]
    core = meta[1]
    wide = SLOTS * HD
    my_lanes = pl.ds(pl.multiple_of(core * wide, wide), wide)
    mine = pl.multiple_of(core * SEQ_ROWS, SEQ_ROWS)
    theirs = pl.multiple_of((1 - core) * SEQ_ROWS, SEQ_ROWS)
    win[0:SEQ_ROWS, :] = prev_ref[...]
    for lanes, inner, outer in both_kinds(meta, here_ref, other_ref, pair_ref, diag_ref):
        win[pl.ds(SEQ_ROWS + mine, SEQ_ROWS), lanes] = inner[...]
        win[pl.ds(SEQ_ROWS + theirs, SEQ_ROWS), lanes] = outer[...]
    q_ref[pl.ds(mine, SEQ_ROWS), :] = here_ref[:, my_lanes]
    q_ref[pl.ds(theirs, SEQ_ROWS), :] = other_ref[:, my_lanes]
    for i in range(PAIR * SLOTS):
        vc[i, :, HD : 2 * HD] = jnp.ones((NS * BT, HD), jnp.bfloat16)
    causal = lax.broadcasted_iota(jnp.int32, (BT, BT), 0) >= lax.broadcasted_iota(
        jnp.int32, (BT, BT), 1
    )

    def unit(step, carry):
        for i in range(PAIR * SLOTS):
            h = i % SLOTS
            local = step * PAIR + i // SLOTS
            offs = [meta[3 + MINE + h * NS + n] for n in range(NS)]
            good = []
            for n in range(NS):
                at = pl.ds(pl.multiple_of((LB + local - offs[n]) * BT, BT), BT)
                rows = slice(n * BT, (n + 1) * BT)
                kc[i, rows, :] = win[at, 0:HD]
                vc[i, rows, 0:HD] = win[at, HD : 2 * HD]
                good.append(first_block + local - offs[n] >= 0)
            rows = pl.ds(pl.multiple_of(local * BT, BT), BT)
            q = q_ref[rows, h * HD : (h + 1) * HD]
            s = lax.dot_general(q, kc[i], DIMS, preferred_element_type=jnp.float32)
            parts = [jnp.where(causal, s[:, 0:BT], NEG)]
            for n in range(1, NS):
                parts.append(s[:, n * BT : (n + 1) * BT] + jnp.where(good[n], 0.0, NEG))
            top = jnp.maximum(jnp.maximum(parts[0], parts[1]), parts[2])
            top = jnp.broadcast_to(jnp.max(top, axis=1, keepdims=True), (BT, HD))
            w = jnp.concatenate(
                [jnp.exp2((x - top) * LOG2E_SCALE).astype(jnp.bfloat16) for x in parts], axis=1
            )
            acc_ref[rows, 2 * h * HD : 2 * (h + 1) * HD] = jnp.dot(
                w, vc[i], preferred_element_type=jnp.float32
            )
            top_ref[rows, h * HD : (h + 1) * HD] = top
        return carry

    lax.fori_loop(0, TOKENS // BT // PAIR, unit, 0)


def near(meta, here, other, pair, diag, prev):
    vm = pl.BlockSpec(memory_space=pltpu.VMEM)
    return pl.pallas_call(
        near_part,
        out_shape=(
            jax.ShapeDtypeStruct((TOKENS, 2 * SLOTS * HD), jnp.float32),
            jax.ShapeDtypeStruct((TOKENS, SLOTS * HD), jnp.float32),
            jax.ShapeDtypeStruct((TOKENS, SLOTS * HD), jnp.bfloat16),
        ),
        in_specs=[pl.BlockSpec(memory_space=pltpu.SMEM), vm, vm, vm, vm, vm],
        out_specs=(vm, vm, vm),
        scratch_shapes=[
            pltpu.VMEM((TOKENS + SEQ_ROWS, 2 * HD), jnp.bfloat16),
            pltpu.VMEM((PAIR * SLOTS, NS * BT, HD), jnp.bfloat16),
            pltpu.VMEM((PAIR * SLOTS, NS * BT, 2 * HD), jnp.bfloat16),
        ],
        name="near",
        compiler_params=pltpu.CompilerParams(vmem_limit_bytes=LARGE),
    )(in_smem(meta), *(in_vmem(x) for x in (here, other, pair, diag, prev)))


def far_part(
    meta, q_hbm, acc_hbm, top_hbm, vert_ref, o_ref, q_ref, acc_ref, top_ref, vk, vv, sems
):
    first_block = meta[0]
    steps = TOKENS // BT // PAIR
    moves = ((q_hbm, q_ref), (top_hbm, top_ref), (acc_hbm, acc_ref))

    def fetch(step):
        rows = pl.ds(pl.multiple_of(step * PAIR * BT, PAIR * BT), PAIR * BT)
        return [
            pltpu.make_async_copy(source.at[rows], target.at[rows], sems.at[n, step])
            for n, (source, target) in enumerate(moves)
        ]

    for step in range(steps):
        for copy in fetch(step):
            copy.start()
    for h in range(SLOTS):
        vv[h, :, HD : 2 * HD] = jnp.ones((NV * BT, HD), jnp.bfloat16)
        for n in range(NV):
            rows = slice(n * BT, (n + 1) * BT)
            for kind, target in ((0, vk), (1, vv)):
                x = vert_ref[:, kind, h * NV + n].astype(jnp.float32).reshape(BT, HD)
                target[h, rows, 0:HD] = x.astype(jnp.bfloat16)

    def unit(step, carry):
        moving = fetch(step)
        moving[0].wait()
        moving[1].wait()
        later = []
        both = pl.ds(pl.multiple_of(step * PAIR * BT, PAIR * BT), PAIR * BT)
        for h in range(SLOTS):
            offs = [meta[3 + MINE + h * NS + n] for n in range(NS)]
            verts = [meta[3 + h * NV + n] for n in range(NV)]
            lane = slice(h * HD, (h + 1) * HD)
            s = lax.dot_general(q_ref[both, lane], vk[h], DIMS, preferred_element_type=jnp.float32)
            ws = []
            keeps = []
            for p in range(PAIR):
                local = step * PAIR + p
                block = first_block + local
                parts = []
                for n in range(NV):
                    ok = verts[n] <= block
                    for o in offs:
                        ok = ok & (block - verts[n] != o)
                    for e in range(n):
                        ok = ok & (verts[n] != verts[e])
                    x = s[p * BT : (p + 1) * BT, n * BT : (n + 1) * BT]
                    parts.append(x + jnp.where(ok, 0.0, NEG))
                rows = pl.ds(pl.multiple_of(local * BT, BT), BT)
                old = top_ref[rows, lane]
                top = jnp.maximum(
                    jnp.maximum(parts[0], parts[1]), jnp.maximum(parts[2], parts[3])
                )
                top = jnp.maximum(
                    jnp.broadcast_to(jnp.max(top, axis=1, keepdims=True), (BT, HD)), old
                )
                keeps.append(jnp.exp2((old - top) * LOG2E_SCALE))
                ws.append(
                    jnp.concatenate(
                        [jnp.exp2((x - top) * LOG2E_SCALE).astype(jnp.bfloat16) for x in parts],
                        axis=1,
                    )
                )
            gain = jnp.dot(
                jnp.concatenate(ws, axis=0), vv[h], preferred_element_type=jnp.float32
            )
            later.append((keeps, gain))
        moving[2].wait()
        for h, (keeps, gain) in enumerate(later):
            lane = slice(h * HD, (h + 1) * HD)
            for p in range(PAIR):
                rows = pl.ds(pl.multiple_of((step * PAIR + p) * BT, BT), BT)
                here = slice(p * BT, (p + 1) * BT)
                acc = acc_ref[rows, 2 * h * HD : (2 * h + 1) * HD] * keeps[p] + gain[here, 0:HD]
                total = (
                    acc_ref[rows, (2 * h + 1) * HD : (2 * h + 2) * HD] * keeps[p]
                    + gain[here, HD : 2 * HD]
                )
                o_ref[rows, lane] = (acc / total).astype(jnp.bfloat16)
        return carry

    lax.fori_loop(0, steps, unit, 0)


def far(meta, q, acc, top, vert):
    vm = pl.BlockSpec(memory_space=pltpu.VMEM)
    hbm = pl.BlockSpec(memory_space=pltpu.HBM)
    return pl.pallas_call(
        far_part,
        out_shape=pltpu.VMEM((TOKENS, SLOTS * HD), jnp.bfloat16),
        in_specs=[pl.BlockSpec(memory_space=pltpu.SMEM), hbm, hbm, hbm, vm],
        out_specs=vm,
        scratch_shapes=[
            pltpu.VMEM((TOKENS, SLOTS * HD), jnp.bfloat16),
            pltpu.VMEM((TOKENS, 2 * SLOTS * HD), jnp.float32),
            pltpu.VMEM((TOKENS, SLOTS * HD), jnp.float32),
            pltpu.VMEM((SLOTS, NV * BT, HD), jnp.bfloat16),
            pltpu.VMEM((SLOTS, NV * BT, 2 * HD), jnp.bfloat16),
            pltpu.SemaphoreType.DMA((3, TOKENS // BT // PAIR)),
        ],
        name="far",
        compiler_params=pltpu.CompilerParams(vmem_limit_bytes=LARGE),
    )(in_smem(meta), in_hbm(q), in_hbm(acc), in_hbm(top), in_vmem(vert))


def cut(here_ref, o_ref, x_ref):
    x_ref[...] = here_ref[:, CHIP_WIDE:WIDE]
    for j in range(LB):
        x = here_ref[j * BT : (j + 1) * BT, CHIP_WIDE:WIDE].astype(jnp.float32)
        for r in range(SUB):
            o_ref[r, j] = x[r * CH : (r + 1) * CH].astype(jnp.bfloat16)


def in_chunks(here):
    vm = pl.BlockSpec(memory_space=pltpu.VMEM)
    return pl.pallas_call(
        cut,
        out_shape=(
            pltpu.VMEM((SUB, LB, CH, HD), jnp.bfloat16),
            pltpu.VMEM((SEQ_ROWS, HD), jnp.bfloat16),
        ),
        in_specs=[vm],
        out_specs=(vm, vm),
        name="cut",
        compiler_params=pltpu.CompilerParams(vmem_limit_bytes=SMALL),
    )(in_vmem(here))


def newest(meta, here_ref, other_ref, pair_ref, diag_ref, o_ref):
    for lanes, inner, outer in both_kinds(meta, here_ref, other_ref, pair_ref, diag_ref):

        @pl.when(meta[1] == 1)
        def _():
            o_ref[:, lanes] = inner[...]

        @pl.when(meta[1] != 1)
        def _():
            o_ref[:, lanes] = outer[...]


def last_window(meta, here, other, pair, diag):
    vm = pl.BlockSpec(memory_space=pltpu.VMEM)
    return pl.pallas_call(
        newest,
        out_shape=pltpu.VMEM((SEQ_ROWS, 2 * HD), jnp.bfloat16),
        in_specs=[pl.BlockSpec(memory_space=pltpu.SMEM), vm, vm, vm, vm],
        out_specs=vm,
        name="newest",
        compiler_params=pltpu.CompilerParams(vmem_limit_bytes=SMALL),
    )(in_smem(meta), *(in_vmem(x) for x in (here, other, pair, diag)))


def choose(spots, held_ref, o_ref):
    for pair in range(2):
        for c in range(CORES):
            for j in range(MINE):
                at = (pair * CORES + c) * MINE + j
                mine = jnp.where(spots[PAIR_SLOTS + at] == 1, 1.0, 0.0).astype(jnp.bfloat16)
                o_ref[at] = held_ref[spots[at]] * mine


def chosen_chunks(spots, held):
    vm = pl.BlockSpec(memory_space=pltpu.VMEM)
    return pl.pallas_call(
        choose,
        out_shape=pltpu.VMEM((PAIR_SLOTS, CH, HD), jnp.bfloat16),
        in_specs=[pl.BlockSpec(memory_space=pltpu.SMEM), vm],
        out_specs=vm,
        name="choose",
        compiler_params=pltpu.CompilerParams(vmem_limit_bytes=SMALL),
    )(in_smem(spots), in_vmem(held))


def add_up(x_ref, one_ref, two_ref, o_ref):
    for pair in range(2):
        for c in range(CORES):
            slots = slice((pair * CORES + c) * MINE, (pair * CORES + c + 1) * MINE)
            total = x_ref[slots] + one_ref[slots] + two_ref[slots]
            for part in range(8):
                o_ref[(part * CORES + c) * 2 + pair] = total


def copies_of_sum(x, one, two):
    vm = pl.BlockSpec(memory_space=pltpu.VMEM)
    return pl.pallas_call(
        add_up,
        out_shape=pltpu.VMEM((8 * CORES * 2, MINE, CH, HD), jnp.bfloat16),
        in_specs=[vm, vm, vm],
        out_specs=vm,
        name="add_up",
        compiler_params=pltpu.CompilerParams(vmem_limit_bytes=SMALL),
    )(in_vmem(x), in_vmem(one), in_vmem(two))


def lay_out(q_ref, k_ref, v_ref, o_ref, sems):
    copies = []
    for g in range(GROUPS):
        m = g // 2 * HD
        for n, (ref, start, at, size) in enumerate(
            (
                (q_ref, g * CHIP_WIDE, 0, CHIP_WIDE),
                (v_ref if g % 2 else k_ref, m, CHIP_WIDE, HD),
            )
        ):
            copies.append(
                pltpu.make_async_copy(
                    ref.at[:, pl.ds(start, size)], o_ref.at[g, :, pl.ds(at, size)], sems.at[n, g]
                )
            )
    for copy in copies:
        copy.start()
    for copy in copies:
        copy.wait()


def pack(q, k, v):
    anywhere = pl.BlockSpec(memory_space=pltpu.HBM)
    return pl.pallas_call(
        lay_out,
        out_shape=pltpu.VMEM((GROUPS, ROWS, WIDE), jnp.bfloat16),
        in_specs=[anywhere] * 3,
        out_specs=pl.BlockSpec(memory_space=pltpu.VMEM),
        scratch_shapes=[pltpu.SemaphoreType.DMA((2, GROUPS))],
        name="lay_out",
        compiler_params=pltpu.CompilerParams(vmem_limit_bytes=SMALL),
    )(in_hbm(q), in_hbm(k), in_hbm(v))


def to_slots(assign, x_ref, o_ref, sems):
    copies = []
    for k in range(QUERY_HEADS):
        a = assign[k]
        source = (a >> 1 & 1) * GROUPS + (a >> 2)
        lane = pl.ds(pl.multiple_of((a & 1) * HD, HD), HD)
        copies.append(
            pltpu.make_async_copy(
                x_ref.at[source, :, lane], o_ref.at[:, pl.ds(k * HD, HD)], sems.at[k]
            )
        )
        copies[-1].start()
    for copy in copies:
        copy.wait()


def place_slots(assign, x):
    return pl.pallas_call(
        to_slots,
        out_shape=jax.ShapeDtypeStruct((ROWS, QUERY_HEADS * HD), jnp.bfloat16),
        in_specs=[
            pl.BlockSpec(memory_space=pltpu.SMEM),
            pl.BlockSpec(memory_space=pltpu.VMEM),
        ],
        out_specs=pl.BlockSpec(memory_space=pl.ANY),
        scratch_shapes=[pltpu.SemaphoreType.DMA((QUERY_HEADS,))],
        name="to_slots",
        compiler_params=pltpu.CompilerParams(vmem_limit_bytes=SMALL),
    )(in_smem(assign), in_vmem(x))


def per_device(q_rows, k_rows, v_rows, group_assign, vertical_blocks, slash_offsets):
    group = lax.axis_index(HEAD)
    core = lax.axis_index("c")
    odd = lax.axis_index("yb")
    chip = lax.axis_index(("xl", "za", "zb"))
    za = lax.axis_index("za")
    pair_heads = 2 * CORES * SLOTS
    verts = lax.dynamic_slice_in_dim(vertical_blocks, group // 2 * pair_heads, pair_heads)
    verts = verts.reshape(-1)
    my_head = (group * CORES + core) * SLOTS
    my_verts = lax.dynamic_slice_in_dim(vertical_blocks, my_head, SLOTS).reshape(-1)
    my_offs = lax.dynamic_slice_in_dim(slash_offsets, my_head, SLOTS).reshape(-1)
    place = jnp.stack([chip * CORES * LB, core, odd]).astype(jnp.int32)
    meta = jnp.concatenate([place, my_verts, my_offs])

    sent = pack(q_rows, k_rows, v_rows)
    here = lax.all_to_all(sent, HEAD, 0, 0, tiled=True).reshape(SEQ_ROWS, WIDE)
    chunks, x_here = in_chunks(here)
    held = lax.all_to_all(chunks, PART, 0, 0, tiled=True)

    other = lax.ppermute(here, "c", [(0, 1), (1, 0)])
    pair = lax.ppermute(x_here, "yb", [(0, 1), (1, 0)])
    diag = lax.ppermute(x_here, ("c", "yb"), [(0, 3), (1, 2), (2, 1), (3, 0)])
    last = last_window(meta, here, other, pair, diag)
    kv_before = lax.ppermute(last, ("xl", "za", "zb"), [(i, i + 1) for i in range(23)])

    owner = verts // LB
    z = (owner % 24) // 2
    spot = ((owner // 24) * 8 + (z % 4) * 2 + owner % 2) * LB + verts % LB
    spots = jnp.concatenate([spot, (z // 4 == za).astype(jnp.int32)])
    chosen = chosen_chunks(spots, held.reshape(SUB * LB, CH, HD))
    one = lax.ppermute(chosen, "za", [(0, 1), (1, 2), (2, 0)])
    two = lax.ppermute(chosen, "za", [(0, 2), (1, 0), (2, 1)])
    spread = copies_of_sum(chosen, one, two)
    vert = lax.all_to_all(spread, ("xl", "zb", "c", "yb"), 0, 0, tiled=True)
    acc, top, q_here = near(meta, here, other, pair, diag, kv_before)
    out = far(meta, q_here, acc, top, vert.reshape(SUB, 2, MINE, CH, HD))
    back = lax.all_to_all(
        out.reshape(CORES * GROUPS, ROWS, SLOTS * HD), SPLIT, 0, 0, tiled=True
    )
    return place_slots(group_assign, back)


def solution(mesh):
    fine = Mesh(mesh.devices.reshape(2, 3, 4, 2, 2, 4, 2), ALL)
    rows = P(ALL, None)
    return jax.shard_map(
        per_device,
        mesh=fine,
        in_specs=(rows, rows, rows, P(), P(), P()),
        out_specs=rows,
        check_vma=False,
    )
```

```python
import math

import jax
import jax.numpy as jnp
from jax import lax
from jax.experimental import pallas as pl
from jax.experimental.pallas import tpu as pltpu
from jax.sharding import Mesh, PartitionSpec as P


QUERY_HEADS = 64
KEY_VALUE_HEADS = 8
HD = 128
BT = 128
NV = 4
NS = 3
GROUPS = 16
CORES = 2
SLOTS = QUERY_HEADS // GROUPS // CORES
ROWS = 40
SEQ_ROWS = 640
LB = SEQ_ROWS // BT
TOKENS = CORES * SEQ_ROWS
CHIP_WIDE = CORES * SLOTS * HD
WIDE = CHIP_WIDE + HD
MINE = SLOTS * NV
PAIR_SLOTS = 2 * CORES * MINE
CH = 8
SUB = 16
ALL = ("xl", "za", "zb", "c", "xh", "ya", "yb")
HEAD = ("xh", "ya", "yb")
SPLIT = ("c", "xh", "ya", "yb")
PART = ("xl", "zb", "c")
SCALE = 1.0 / math.sqrt(HD)
NEG = float("-inf")
SMALL = 4 * 1024 * 1024
PAIR = 5
LARGE = 12 * 1024 * 1024


LOG2E_SCALE = SCALE * math.log2(math.e)
DIMS = (((1,), (1,)), ((), ()))


def in_vmem(x):
    return pltpu.with_memory_space_constraint(x, pltpu.VMEM)


def in_smem(x):
    return pltpu.with_memory_space_constraint(x, pltpu.SMEM)


def in_hbm(x):
    return pltpu.with_memory_space_constraint(x, pltpu.HBM)


def both_kinds(meta, here_ref, other_ref, pair_ref):
    own = pl.ds(pl.multiple_of(meta[2] * HD, HD), HD)
    rest = pl.ds(pl.multiple_of((1 - meta[2]) * HD, HD), HD)
    x = slice(CHIP_WIDE, WIDE)
    return (
        (own, here_ref.at[:, x], other_ref.at[:, x]),
        (rest, pair_ref.at[0:SEQ_ROWS], pair_ref.at[SEQ_ROWS:TOKENS]),
    )


def near_part(
    meta,
    here_ref,
    other_ref,
    pair_ref,
    prev_ref,
    acc_hbm,
    top_hbm,
    q_hbm,
    acc_ref,
    top_ref,
    q_ref,
    win,
    kc,
    vc,
    sems,
):
    first_block = meta[0]
    core = meta[1]
    wide = SLOTS * HD
    my_lanes = pl.ds(pl.multiple_of(core * wide, wide), wide)
    mine = pl.multiple_of(core * SEQ_ROWS, SEQ_ROWS)
    theirs = pl.multiple_of((1 - core) * SEQ_ROWS, SEQ_ROWS)
    win[0:SEQ_ROWS, :] = prev_ref[...]
    for lanes, inner, outer in both_kinds(meta, here_ref, other_ref, pair_ref):
        win[pl.ds(SEQ_ROWS + mine, SEQ_ROWS), lanes] = inner[...]
        win[pl.ds(SEQ_ROWS + theirs, SEQ_ROWS), lanes] = outer[...]
    q_ref[pl.ds(mine, SEQ_ROWS), :] = here_ref[:, my_lanes]
    q_ref[pl.ds(theirs, SEQ_ROWS), :] = other_ref[:, my_lanes]
    steps = TOKENS // BT // PAIR
    whole = pltpu.make_async_copy(q_ref, q_hbm, sems.at[2, 0])
    whole.start()

    def put(step):
        rows = pl.ds(pl.multiple_of(step * PAIR * BT, PAIR * BT), PAIR * BT)
        return [
            pltpu.make_async_copy(source.at[rows], target.at[rows], sems.at[n, step])
            for n, (source, target) in enumerate(((acc_ref, acc_hbm), (top_ref, top_hbm)))
        ]

    for i in range(PAIR * SLOTS):
        vc[i, :, HD : 2 * HD] = jnp.ones((NS * BT, HD), jnp.bfloat16)
    causal = lax.broadcasted_iota(jnp.int32, (BT, BT), 0) >= lax.broadcasted_iota(
        jnp.int32, (BT, BT), 1
    )

    def unit(step, carry):
        for i in range(PAIR * SLOTS):
            h = i % SLOTS
            local = step * PAIR + i // SLOTS
            offs = [meta[3 + MINE + h * NS + n] for n in range(NS)]
            good = []
            for n in range(NS):
                at = pl.ds(pl.multiple_of((LB + local - offs[n]) * BT, BT), BT)
                rows = slice(n * BT, (n + 1) * BT)
                kc[i, rows, :] = win[at, 0:HD]
                vc[i, rows, 0:HD] = win[at, HD : 2 * HD]
                good.append(first_block + local - offs[n] >= 0)
            rows = pl.ds(pl.multiple_of(local * BT, BT), BT)
            q = q_ref[rows, h * HD : (h + 1) * HD]
            s = lax.dot_general(q, kc[i], DIMS, preferred_element_type=jnp.float32)
            parts = [jnp.where(causal, s[:, 0:BT], NEG)]
            for n in range(1, NS):
                parts.append(s[:, n * BT : (n + 1) * BT] + jnp.where(good[n], 0.0, NEG))
            top = jnp.maximum(jnp.maximum(parts[0], parts[1]), parts[2])
            top = jnp.broadcast_to(jnp.max(top, axis=1, keepdims=True), (BT, HD))
            w = jnp.concatenate(
                [jnp.exp2((x - top) * LOG2E_SCALE).astype(jnp.bfloat16) for x in parts], axis=1
            )
            acc_ref[rows, 2 * h * HD : 2 * (h + 1) * HD] = jnp.dot(
                w, vc[i], preferred_element_type=jnp.float32
            )
            top_ref[rows, h * HD : (h + 1) * HD] = top
        for copy in put(step):
            copy.start()
        return carry

    lax.fori_loop(0, steps, unit, 0)
    whole.wait()
    for step in range(steps):
        for copy in put(step):
            copy.wait()


def near(meta, here, other, pair, prev):
    vm = pl.BlockSpec(memory_space=pltpu.VMEM)
    return pl.pallas_call(
        near_part,
        out_shape=(
            pltpu.HBM((TOKENS, 2 * SLOTS * HD), jnp.float32),
            pltpu.HBM((TOKENS, SLOTS * HD), jnp.float32),
            pltpu.HBM((TOKENS, SLOTS * HD), jnp.bfloat16),
        ),
        in_specs=[pl.BlockSpec(memory_space=pltpu.SMEM), vm, vm, vm, vm],
        out_specs=tuple(pl.BlockSpec(memory_space=pltpu.HBM) for _ in range(3)),
        scratch_shapes=[
            pltpu.VMEM((TOKENS, 2 * SLOTS * HD), jnp.float32),
            pltpu.VMEM((TOKENS, SLOTS * HD), jnp.float32),
            pltpu.VMEM((TOKENS, SLOTS * HD), jnp.bfloat16),
            pltpu.VMEM((TOKENS + SEQ_ROWS, 2 * HD), jnp.bfloat16),
            pltpu.VMEM((PAIR * SLOTS, NS * BT, HD), jnp.bfloat16),
            pltpu.VMEM((PAIR * SLOTS, NS * BT, 2 * HD), jnp.bfloat16),
            pltpu.SemaphoreType.DMA((3, TOKENS // BT // PAIR)),
        ],
        name="near",
        compiler_params=pltpu.CompilerParams(vmem_limit_bytes=LARGE),
    )(in_smem(meta), *(in_vmem(x) for x in (here, other, pair, prev)))


def far_part(
    meta, q_hbm, acc_hbm, top_hbm, vert_ref, o_ref, q_ref, acc_ref, top_ref, vk, vv, sems
):
    first_block = meta[0]
    steps = TOKENS // BT // PAIR
    moves = ((q_hbm, q_ref), (top_hbm, top_ref), (acc_hbm, acc_ref))

    def fetch(step):
        rows = pl.ds(pl.multiple_of(step * PAIR * BT, PAIR * BT), PAIR * BT)
        return [
            pltpu.make_async_copy(source.at[rows], target.at[rows], sems.at[n, step])
            for n, (source, target) in enumerate(moves)
        ]

    for step in range(steps):
        for copy in fetch(step):
            copy.start()
    for h in range(SLOTS):
        vv[h, :, HD : 2 * HD] = jnp.ones((NV * BT, HD), jnp.bfloat16)
        for n in range(NV):
            rows = slice(n * BT, (n + 1) * BT)
            for kind, target in ((0, vk), (1, vv)):
                x = vert_ref[:, kind, h * NV + n].astype(jnp.float32).reshape(BT, HD)
                target[h, rows, 0:HD] = x.astype(jnp.bfloat16)

    def unit(step, carry):
        moving = fetch(step)
        moving[0].wait()
        moving[1].wait()
        later = []
        both = pl.ds(pl.multiple_of(step * PAIR * BT, PAIR * BT), PAIR * BT)
        for h in range(SLOTS):
            offs = [meta[3 + MINE + h * NS + n] for n in range(NS)]
            verts = [meta[3 + h * NV + n] for n in range(NV)]
            lane = slice(h * HD, (h + 1) * HD)
            s = lax.dot_general(q_ref[both, lane], vk[h], DIMS, preferred_element_type=jnp.float32)
            ws = []
            keeps = []
            for p in range(PAIR):
                local = step * PAIR + p
                block = first_block + local
                parts = []
                for n in range(NV):
                    ok = verts[n] <= block
                    for o in offs:
                        ok = ok & (block - verts[n] != o)
                    for e in range(n):
                        ok = ok & (verts[n] != verts[e])
                    x = s[p * BT : (p + 1) * BT, n * BT : (n + 1) * BT]
                    parts.append(x + jnp.where(ok, 0.0, NEG))
                rows = pl.ds(pl.multiple_of(local * BT, BT), BT)
                old = top_ref[rows, lane]
                top = jnp.maximum(
                    jnp.maximum(parts[0], parts[1]), jnp.maximum(parts[2], parts[3])
                )
                top = jnp.maximum(
                    jnp.broadcast_to(jnp.max(top, axis=1, keepdims=True), (BT, HD)), old
                )
                keeps.append(jnp.exp2((old - top) * LOG2E_SCALE))
                ws.append(
                    jnp.concatenate(
                        [jnp.exp2((x - top) * LOG2E_SCALE).astype(jnp.bfloat16) for x in parts],
                        axis=1,
                    )
                )
            gain = jnp.dot(
                jnp.concatenate(ws, axis=0), vv[h], preferred_element_type=jnp.float32
            )
            later.append((keeps, gain))
        moving[2].wait()
        for h, (keeps, gain) in enumerate(later):
            lane = slice(h * HD, (h + 1) * HD)
            for p in range(PAIR):
                rows = pl.ds(pl.multiple_of((step * PAIR + p) * BT, BT), BT)
                here = slice(p * BT, (p + 1) * BT)
                acc = acc_ref[rows, 2 * h * HD : (2 * h + 1) * HD] * keeps[p] + gain[here, 0:HD]
                total = (
                    acc_ref[rows, (2 * h + 1) * HD : (2 * h + 2) * HD] * keeps[p]
                    + gain[here, HD : 2 * HD]
                )
                o_ref[rows, lane] = (acc / total).astype(jnp.bfloat16)
        return carry

    lax.fori_loop(0, steps, unit, 0)


def far(meta, q, acc, top, vert):
    vm = pl.BlockSpec(memory_space=pltpu.VMEM)
    hbm = pl.BlockSpec(memory_space=pltpu.HBM)
    return pl.pallas_call(
        far_part,
        out_shape=pltpu.VMEM((TOKENS, SLOTS * HD), jnp.bfloat16),
        in_specs=[pl.BlockSpec(memory_space=pltpu.SMEM), hbm, hbm, hbm, vm],
        out_specs=vm,
        scratch_shapes=[
            pltpu.VMEM((TOKENS, SLOTS * HD), jnp.bfloat16),
            pltpu.VMEM((TOKENS, 2 * SLOTS * HD), jnp.float32),
            pltpu.VMEM((TOKENS, SLOTS * HD), jnp.float32),
            pltpu.VMEM((SLOTS, NV * BT, HD), jnp.bfloat16),
            pltpu.VMEM((SLOTS, NV * BT, 2 * HD), jnp.bfloat16),
            pltpu.SemaphoreType.DMA((3, TOKENS // BT // PAIR)),
        ],
        name="far",
        compiler_params=pltpu.CompilerParams(vmem_limit_bytes=LARGE),
    )(in_smem(meta), in_hbm(q), in_hbm(acc), in_hbm(top), in_vmem(vert))


def cut(here_ref, o_ref):
    for j in range(LB):
        x = here_ref[j * BT : (j + 1) * BT, CHIP_WIDE:WIDE].astype(jnp.float32)
        for r in range(SUB):
            o_ref[r, j] = x[r * CH : (r + 1) * CH].astype(jnp.bfloat16)


def in_chunks(here):
    vm = pl.BlockSpec(memory_space=pltpu.VMEM)
    return pl.pallas_call(
        cut,
        out_shape=pltpu.VMEM((SUB, LB, CH, HD), jnp.bfloat16),
        in_specs=[vm],
        out_specs=vm,
        name="cut",
        compiler_params=pltpu.CompilerParams(vmem_limit_bytes=SMALL),
    )(in_vmem(here))


def stack(here_ref, other_ref, o_ref):
    o_ref[0:SEQ_ROWS, :] = here_ref[:, CHIP_WIDE:WIDE]
    o_ref[SEQ_ROWS:TOKENS, :] = other_ref[:, CHIP_WIDE:WIDE]


def both_windows(here, other):
    vm = pl.BlockSpec(memory_space=pltpu.VMEM)
    return pl.pallas_call(
        stack,
        out_shape=pltpu.VMEM((TOKENS, HD), jnp.bfloat16),
        in_specs=[vm, vm],
        out_specs=vm,
        name="stack",
        compiler_params=pltpu.CompilerParams(vmem_limit_bytes=SMALL),
    )(in_vmem(here), in_vmem(other))


def newest(meta, here_ref, other_ref, pair_ref, o_ref):
    for lanes, inner, outer in both_kinds(meta, here_ref, other_ref, pair_ref):

        @pl.when(meta[1] == 1)
        def _():
            o_ref[:, lanes] = inner[...]

        @pl.when(meta[1] != 1)
        def _():
            o_ref[:, lanes] = outer[...]


def last_window(meta, here, other, pair):
    vm = pl.BlockSpec(memory_space=pltpu.VMEM)
    return pl.pallas_call(
        newest,
        out_shape=pltpu.VMEM((SEQ_ROWS, 2 * HD), jnp.bfloat16),
        in_specs=[pl.BlockSpec(memory_space=pltpu.SMEM), vm, vm, vm],
        out_specs=vm,
        name="newest",
        compiler_params=pltpu.CompilerParams(vmem_limit_bytes=SMALL),
    )(in_smem(meta), *(in_vmem(x) for x in (here, other, pair)))


def choose(spots, held_ref, o_ref):
    for pair in range(2):
        for c in range(CORES):
            for j in range(MINE):
                at = (pair * CORES + c) * MINE + j
                mine = jnp.where(spots[PAIR_SLOTS + at] == 1, 1.0, 0.0).astype(jnp.bfloat16)
                o_ref[at] = held_ref[spots[at]] * mine


def chosen_chunks(spots, held):
    vm = pl.BlockSpec(memory_space=pltpu.VMEM)
    return pl.pallas_call(
        choose,
        out_shape=pltpu.VMEM((PAIR_SLOTS, CH, HD), jnp.bfloat16),
        in_specs=[pl.BlockSpec(memory_space=pltpu.SMEM), vm],
        out_specs=vm,
        name="choose",
        compiler_params=pltpu.CompilerParams(vmem_limit_bytes=SMALL),
    )(in_smem(spots), in_vmem(held))


def add_up(x_ref, one_ref, two_ref, o_ref):
    for pair in range(2):
        for c in range(CORES):
            slots = slice((pair * CORES + c) * MINE, (pair * CORES + c + 1) * MINE)
            total = x_ref[slots] + one_ref[slots] + two_ref[slots]
            for part in range(8):
                o_ref[(part * CORES + c) * 2 + pair] = total


def copies_of_sum(x, one, two):
    vm = pl.BlockSpec(memory_space=pltpu.VMEM)
    return pl.pallas_call(
        add_up,
        out_shape=pltpu.VMEM((8 * CORES * 2, MINE, CH, HD), jnp.bfloat16),
        in_specs=[vm, vm, vm],
        out_specs=vm,
        name="add_up",
        compiler_params=pltpu.CompilerParams(vmem_limit_bytes=SMALL),
    )(in_vmem(x), in_vmem(one), in_vmem(two))


def lay_out(q_hbm, k_hbm, v_hbm, o_ref, q_ref, k_ref, v_ref, sems):
    step = 8
    copies = [
        pltpu.make_async_copy(k_hbm, k_ref, sems.at[0]),
        pltpu.make_async_copy(v_hbm, v_ref, sems.at[1]),
    ]
    for n, row in enumerate(range(0, ROWS, step)):
        rows = pl.ds(row, step)
        copies.append(pltpu.make_async_copy(q_hbm.at[rows], q_ref.at[rows], sems.at[2 + n]))
    for copy in copies:
        copy.start()
    copies[0].wait()
    copies[1].wait()
    for g in range(GROUPS):
        m = g // 2 * HD
        o_ref[g, :, CHIP_WIDE:WIDE] = (v_ref if g % 2 else k_ref)[:, m : m + HD]
    for n, row in enumerate(range(0, ROWS, step)):
        copies[2 + n].wait()
        for g in range(GROUPS):
            o_ref[g, row : row + step, 0:CHIP_WIDE] = q_ref[
                row : row + step, g * CHIP_WIDE : (g + 1) * CHIP_WIDE
            ]


def pack(q, k, v):
    return pl.pallas_call(
        lay_out,
        out_shape=pltpu.VMEM((GROUPS, ROWS, WIDE), jnp.bfloat16),
        in_specs=[pl.BlockSpec(memory_space=pltpu.HBM)] * 3,
        out_specs=pl.BlockSpec(memory_space=pltpu.VMEM),
        scratch_shapes=[
            pltpu.VMEM((ROWS, QUERY_HEADS * HD), jnp.bfloat16),
            pltpu.VMEM((ROWS, KEY_VALUE_HEADS * HD), jnp.bfloat16),
            pltpu.VMEM((ROWS, KEY_VALUE_HEADS * HD), jnp.bfloat16),
            pltpu.SemaphoreType.DMA((2 + ROWS // 8,)),
        ],
        name="lay_out",
        compiler_params=pltpu.CompilerParams(vmem_limit_bytes=SMALL),
    )(in_hbm(q), in_hbm(k), in_hbm(v))


def to_slots(assign, x_ref, o_ref, sems):
    copies = []
    for k in range(QUERY_HEADS):
        a = assign[k]
        source = (a >> 1 & 1) * GROUPS + (a >> 2)
        lane = pl.ds(pl.multiple_of((a & 1) * HD, HD), HD)
        copies.append(
            pltpu.make_async_copy(
                x_ref.at[source, :, lane], o_ref.at[:, pl.ds(k * HD, HD)], sems.at[k]
            )
        )
        copies[-1].start()
    for copy in copies:
        copy.wait()


def place_slots(assign, x):
    return pl.pallas_call(
        to_slots,
        out_shape=jax.ShapeDtypeStruct((ROWS, QUERY_HEADS * HD), jnp.bfloat16),
        in_specs=[
            pl.BlockSpec(memory_space=pltpu.SMEM),
            pl.BlockSpec(memory_space=pltpu.VMEM),
        ],
        out_specs=pl.BlockSpec(memory_space=pl.ANY),
        scratch_shapes=[pltpu.SemaphoreType.DMA((QUERY_HEADS,))],
        name="to_slots",
        compiler_params=pltpu.CompilerParams(vmem_limit_bytes=SMALL),
    )(in_smem(assign), in_vmem(x))


def per_device(q_rows, k_rows, v_rows, group_assign, vertical_blocks, slash_offsets):
    group = lax.axis_index(HEAD)
    core = lax.axis_index("c")
    odd = lax.axis_index("yb")
    chip = lax.axis_index(("xl", "za", "zb"))
    za = lax.axis_index("za")
    pair_heads = 2 * CORES * SLOTS
    verts = lax.dynamic_slice_in_dim(vertical_blocks, group // 2 * pair_heads, pair_heads)
    verts = verts.reshape(-1)
    my_head = (group * CORES + core) * SLOTS
    my_verts = lax.dynamic_slice_in_dim(vertical_blocks, my_head, SLOTS).reshape(-1)
    my_offs = lax.dynamic_slice_in_dim(slash_offsets, my_head, SLOTS).reshape(-1)
    place = jnp.stack([chip * CORES * LB, core, odd]).astype(jnp.int32)
    meta = jnp.concatenate([place, my_verts, my_offs])

    sent = pack(q_rows, k_rows, v_rows)
    here = lax.all_to_all(sent, HEAD, 0, 0, tiled=True).reshape(SEQ_ROWS, WIDE)
    held = lax.all_to_all(in_chunks(here), PART, 0, 0, tiled=True)

    other = lax.ppermute(here, "c", [(0, 1), (1, 0)])
    windows = both_windows(here, other)
    pair = lax.ppermute(windows, "yb", [(0, 1), (1, 0)])
    last = last_window(meta, here, other, pair)
    kv_before = lax.ppermute(last, ("xl", "za", "zb"), [(i, i + 1) for i in range(23)])

    owner = verts // LB
    z = (owner % 24) // 2
    spot = ((owner // 24) * 8 + (z % 4) * 2 + owner % 2) * LB + verts % LB
    spots = jnp.concatenate([spot, (z // 4 == za).astype(jnp.int32)])
    chosen = chosen_chunks(spots, held.reshape(SUB * LB, CH, HD))
    one = lax.ppermute(chosen, "za", [(0, 1), (1, 2), (2, 0)])
    two = lax.ppermute(chosen, "za", [(0, 2), (1, 0), (2, 1)])
    spread = copies_of_sum(chosen, one, two)
    vert = lax.all_to_all(spread, ("xl", "zb", "c", "yb"), 0, 0, tiled=True)
    acc, top, q_here = near(meta, here, other, pair, kv_before)
    out = far(meta, q_here, acc, top, vert.reshape(SUB, 2, MINE, CH, HD))
    back = lax.all_to_all(
        out.reshape(CORES * GROUPS, ROWS, SLOTS * HD), SPLIT, 0, 0, tiled=True
    )
    return place_slots(group_assign, back)


def solution(mesh):
    fine = Mesh(mesh.devices.reshape(2, 3, 4, 2, 2, 4, 2), ALL)
    rows = P(ALL, None)
    return jax.shard_map(
        per_device,
        mesh=fine,
        in_specs=(rows, rows, rows, P(), P(), P()),
        out_specs=rows,
        check_vma=False,
    )
```

```python
import math

import jax
import jax.numpy as jnp
from jax import lax
from jax.experimental import pallas as pl
from jax.experimental.pallas import tpu as pltpu
from jax.sharding import Mesh, PartitionSpec as P


QUERY_HEADS = 64
KEY_VALUE_HEADS = 8
HD = 128
BT = 128
NV = 4
NS = 3
GROUPS = 16
CORES = 2
SLOTS = QUERY_HEADS // GROUPS // CORES
ROWS = 40
SEQ_ROWS = 640
LB = SEQ_ROWS // BT
TOKENS = CORES * SEQ_ROWS
CHIP_WIDE = CORES * SLOTS * HD
WIDE = CHIP_WIDE + HD
MINE = SLOTS * NV
CH = 8
PARTS = 3
SUB = 16
ALL = ("xl", "za", "zb", "c", "xh", "ya", "yb")
SEQ = ("xl", "za", "zb", "c")
HEAD = ("xh", "ya", "yb")
SPLIT = ("c", "xh", "ya", "yb")
SCALE = 1.0 / math.sqrt(HD)
NEG = float("-inf")
SMALL = 4 * 1024 * 1024
PAIR = 5
LARGE = 12 * 1024 * 1024


LOG2E_SCALE = SCALE * math.log2(math.e)
DIMS = (((1,), (1,)), ((), ()))


def in_vmem(x):
    return pltpu.with_memory_space_constraint(x, pltpu.VMEM)


def in_smem(x):
    return pltpu.with_memory_space_constraint(x, pltpu.SMEM)


def in_hbm(x):
    return pltpu.with_memory_space_constraint(x, pltpu.HBM)


def both_kinds(meta, here_ref, other_ref, pair_ref, diag_ref):
    own = pl.ds(pl.multiple_of(meta[2] * HD, HD), HD)
    rest = pl.ds(pl.multiple_of((1 - meta[2]) * HD, HD), HD)
    x = slice(CHIP_WIDE, WIDE)
    return ((own, here_ref.at[:, x], other_ref.at[:, x]), (rest, pair_ref, diag_ref))


def near_part(
    meta,
    here_ref,
    other_ref,
    pair_ref,
    diag_ref,
    prev_ref,
    acc_hbm,
    top_hbm,
    q_hbm,
    acc_ref,
    top_ref,
    q_ref,
    win,
    kc,
    vc,
    sems,
):
    first_block = meta[0]
    core = meta[1]
    wide = SLOTS * HD
    my_lanes = pl.ds(pl.multiple_of(core * wide, wide), wide)
    mine = pl.multiple_of(core * SEQ_ROWS, SEQ_ROWS)
    theirs = pl.multiple_of((1 - core) * SEQ_ROWS, SEQ_ROWS)
    win[0:SEQ_ROWS, :] = prev_ref[...]
    for lanes, inner, outer in both_kinds(meta, here_ref, other_ref, pair_ref, diag_ref):
        win[pl.ds(SEQ_ROWS + mine, SEQ_ROWS), lanes] = inner[...]
        win[pl.ds(SEQ_ROWS + theirs, SEQ_ROWS), lanes] = outer[...]
    q_ref[pl.ds(mine, SEQ_ROWS), :] = here_ref[:, my_lanes]
    q_ref[pl.ds(theirs, SEQ_ROWS), :] = other_ref[:, my_lanes]
    steps = TOKENS // BT // PAIR
    whole = pltpu.make_async_copy(q_ref, q_hbm, sems.at[2, 0])
    whole.start()

    def put(step):
        rows = pl.ds(pl.multiple_of(step * PAIR * BT, PAIR * BT), PAIR * BT)
        return [
            pltpu.make_async_copy(source.at[rows], target.at[rows], sems.at[n, step])
            for n, (source, target) in enumerate(((acc_ref, acc_hbm), (top_ref, top_hbm)))
        ]

    for i in range(PAIR * SLOTS):
        vc[i, :, HD : 2 * HD] = jnp.ones((NS * BT, HD), jnp.bfloat16)
    causal = lax.broadcasted_iota(jnp.int32, (BT, BT), 0) >= lax.broadcasted_iota(
        jnp.int32, (BT, BT), 1
    )

    def unit(step, carry):
        for i in range(PAIR * SLOTS):
            h = i % SLOTS
            local = step * PAIR + i // SLOTS
            offs = [meta[3 + MINE + h * NS + n] for n in range(NS)]
            good = []
            for n in range(NS):
                at = pl.ds(pl.multiple_of((LB + local - offs[n]) * BT, BT), BT)
                rows = slice(n * BT, (n + 1) * BT)
                kc[i, rows, :] = win[at, 0:HD]
                vc[i, rows, 0:HD] = win[at, HD : 2 * HD]
                good.append(first_block + local - offs[n] >= 0)
            rows = pl.ds(pl.multiple_of(local * BT, BT), BT)
            q = q_ref[rows, h * HD : (h + 1) * HD]
            s = lax.dot_general(q, kc[i], DIMS, preferred_element_type=jnp.float32)
            parts = [jnp.where(causal, s[:, 0:BT], NEG)]
            for n in range(1, NS):
                parts.append(s[:, n * BT : (n + 1) * BT] + jnp.where(good[n], 0.0, NEG))
            top = jnp.maximum(jnp.maximum(parts[0], parts[1]), parts[2])
            top = jnp.broadcast_to(jnp.max(top, axis=1, keepdims=True), (BT, HD))
            w = jnp.concatenate(
                [jnp.exp2((x - top) * LOG2E_SCALE).astype(jnp.bfloat16) for x in parts], axis=1
            )
            acc_ref[rows, 2 * h * HD : 2 * (h + 1) * HD] = jnp.dot(
                w, vc[i], preferred_element_type=jnp.float32
            )
            top_ref[rows, h * HD : (h + 1) * HD] = top
        for copy in put(step):
            copy.start()
        return carry

    lax.fori_loop(0, steps, unit, 0)
    whole.wait()
    for step in range(steps):
        for copy in put(step):
            copy.wait()


def near(meta, here, other, pair, diag, prev):
    vm = pl.BlockSpec(memory_space=pltpu.VMEM)
    return pl.pallas_call(
        near_part,
        out_shape=(
            pltpu.HBM((TOKENS, 2 * SLOTS * HD), jnp.float32),
            pltpu.HBM((TOKENS, SLOTS * HD), jnp.float32),
            pltpu.HBM((TOKENS, SLOTS * HD), jnp.bfloat16),
        ),
        in_specs=[pl.BlockSpec(memory_space=pltpu.SMEM), vm, vm, vm, vm, vm],
        out_specs=tuple(pl.BlockSpec(memory_space=pltpu.HBM) for _ in range(3)),
        scratch_shapes=[
            pltpu.VMEM((TOKENS, 2 * SLOTS * HD), jnp.float32),
            pltpu.VMEM((TOKENS, SLOTS * HD), jnp.float32),
            pltpu.VMEM((TOKENS, SLOTS * HD), jnp.bfloat16),
            pltpu.VMEM((TOKENS + SEQ_ROWS, 2 * HD), jnp.bfloat16),
            pltpu.VMEM((PAIR * SLOTS, NS * BT, HD), jnp.bfloat16),
            pltpu.VMEM((PAIR * SLOTS, NS * BT, 2 * HD), jnp.bfloat16),
            pltpu.SemaphoreType.DMA((3, TOKENS // BT // PAIR)),
        ],
        name="near",
        compiler_params=pltpu.CompilerParams(vmem_limit_bytes=LARGE),
    )(in_smem(meta), *(in_vmem(x) for x in (here, other, pair, diag, prev)))


def far_part(
    meta, q_hbm, acc_hbm, top_hbm, vert_ref, o_ref, q_ref, acc_ref, top_ref, vk, vv, sems
):
    first_block = meta[0]
    steps = TOKENS // BT // PAIR
    moves = ((q_hbm, q_ref), (top_hbm, top_ref), (acc_hbm, acc_ref))

    def fetch(step):
        rows = pl.ds(pl.multiple_of(step * PAIR * BT, PAIR * BT), PAIR * BT)
        return [
            pltpu.make_async_copy(source.at[rows], target.at[rows], sems.at[n, step])
            for n, (source, target) in enumerate(moves)
        ]

    for step in range(steps):
        for copy in fetch(step):
            copy.start()
    for h in range(SLOTS):
        vv[h, :, HD : 2 * HD] = jnp.ones((NV * BT, HD), jnp.bfloat16)
        for n in range(NV):
            rows = slice(n * BT, (n + 1) * BT)
            for kind, target in ((0, vk), (1, vv)):
                x = vert_ref[:, kind, h * NV + n].astype(jnp.float32).reshape(BT, HD)
                target[h, rows, 0:HD] = x.astype(jnp.bfloat16)

    def unit(step, carry):
        moving = fetch(step)
        moving[0].wait()
        moving[1].wait()
        later = []
        both = pl.ds(pl.multiple_of(step * PAIR * BT, PAIR * BT), PAIR * BT)
        for h in range(SLOTS):
            offs = [meta[3 + MINE + h * NS + n] for n in range(NS)]
            verts = [meta[3 + h * NV + n] for n in range(NV)]
            lane = slice(h * HD, (h + 1) * HD)
            s = lax.dot_general(q_ref[both, lane], vk[h], DIMS, preferred_element_type=jnp.float32)
            ws = []
            keeps = []
            for p in range(PAIR):
                local = step * PAIR + p
                block = first_block + local
                parts = []
                for n in range(NV):
                    ok = verts[n] <= block
                    for o in offs:
                        ok = ok & (block - verts[n] != o)
                    for e in range(n):
                        ok = ok & (verts[n] != verts[e])
                    x = s[p * BT : (p + 1) * BT, n * BT : (n + 1) * BT]
                    parts.append(x + jnp.where(ok, 0.0, NEG))
                rows = pl.ds(pl.multiple_of(local * BT, BT), BT)
                old = top_ref[rows, lane]
                top = jnp.maximum(
                    jnp.maximum(parts[0], parts[1]), jnp.maximum(parts[2], parts[3])
                )
                top = jnp.maximum(
                    jnp.broadcast_to(jnp.max(top, axis=1, keepdims=True), (BT, HD)), old
                )
                keeps.append(jnp.exp2((old - top) * LOG2E_SCALE))
                ws.append(
                    jnp.concatenate(
                        [jnp.exp2((x - top) * LOG2E_SCALE).astype(jnp.bfloat16) for x in parts],
                        axis=1,
                    )
                )
            gain = jnp.dot(
                jnp.concatenate(ws, axis=0), vv[h], preferred_element_type=jnp.float32
            )
            later.append((keeps, gain))
        moving[2].wait()
        for h, (keeps, gain) in enumerate(later):
            lane = slice(h * HD, (h + 1) * HD)
            for p in range(PAIR):
                rows = pl.ds(pl.multiple_of((step * PAIR + p) * BT, BT), BT)
                here = slice(p * BT, (p + 1) * BT)
                acc = acc_ref[rows, 2 * h * HD : (2 * h + 1) * HD] * keeps[p] + gain[here, 0:HD]
                total = (
                    acc_ref[rows, (2 * h + 1) * HD : (2 * h + 2) * HD] * keeps[p]
                    + gain[here, HD : 2 * HD]
                )
                o_ref[rows, lane] = (acc / total).astype(jnp.bfloat16)
        return carry

    lax.fori_loop(0, steps, unit, 0)


def far(meta, q, acc, top, vert):
    vm = pl.BlockSpec(memory_space=pltpu.VMEM)
    hbm = pl.BlockSpec(memory_space=pltpu.HBM)
    return pl.pallas_call(
        far_part,
        out_shape=pltpu.VMEM((TOKENS, SLOTS * HD), jnp.bfloat16),
        in_specs=[pl.BlockSpec(memory_space=pltpu.SMEM), hbm, hbm, hbm, vm],
        out_specs=vm,
        scratch_shapes=[
            pltpu.VMEM((TOKENS, SLOTS * HD), jnp.bfloat16),
            pltpu.VMEM((TOKENS, 2 * SLOTS * HD), jnp.float32),
            pltpu.VMEM((TOKENS, SLOTS * HD), jnp.float32),
            pltpu.VMEM((SLOTS, NV * BT, HD), jnp.bfloat16),
            pltpu.VMEM((SLOTS, NV * BT, 2 * HD), jnp.bfloat16),
            pltpu.SemaphoreType.DMA((3, TOKENS // BT // PAIR)),
        ],
        name="far",
        compiler_params=pltpu.CompilerParams(vmem_limit_bytes=LARGE),
    )(in_smem(meta), in_hbm(q), in_hbm(acc), in_hbm(top), in_vmem(vert))


def cut(here_ref, o_ref, x_ref):
    x_ref[...] = here_ref[:, CHIP_WIDE:WIDE]
    for j in range(LB):
        x = here_ref[j * BT : (j + 1) * BT, CHIP_WIDE:WIDE].astype(jnp.float32)
        for r in range(SUB):
            chunk = x[r * CH : (r + 1) * CH].astype(jnp.bfloat16)
            for part in range(PARTS):
                o_ref[r // 8 * 8 * PARTS + part * 8 + r % 8, j] = chunk


def in_chunks(here):
    vm = pl.BlockSpec(memory_space=pltpu.VMEM)
    return pl.pallas_call(
        cut,
        out_shape=(
            pltpu.VMEM((SUB * PARTS, LB, CH, HD), jnp.bfloat16),
            pltpu.VMEM((SEQ_ROWS, HD), jnp.bfloat16),
        ),
        in_specs=[vm],
        out_specs=(vm, vm),
        name="cut",
        compiler_params=pltpu.CompilerParams(vmem_limit_bytes=SMALL),
    )(in_vmem(here))


def newest(meta, here_ref, other_ref, pair_ref, diag_ref, o_ref):
    for lanes, inner, outer in both_kinds(meta, here_ref, other_ref, pair_ref, diag_ref):

        @pl.when(meta[1] == 1)
        def _():
            o_ref[:, lanes] = inner[...]

        @pl.when(meta[1] != 1)
        def _():
            o_ref[:, lanes] = outer[...]


def last_window(meta, here, other, pair, diag):
    vm = pl.BlockSpec(memory_space=pltpu.VMEM)
    return pl.pallas_call(
        newest,
        out_shape=pltpu.VMEM((SEQ_ROWS, 2 * HD), jnp.bfloat16),
        in_specs=[pl.BlockSpec(memory_space=pltpu.SMEM), vm, vm, vm, vm],
        out_specs=vm,
        name="newest",
        compiler_params=pltpu.CompilerParams(vmem_limit_bytes=SMALL),
    )(in_smem(meta), *(in_vmem(x) for x in (here, other, pair, diag)))


def choose(verts, held_ref, o_ref):
    for pair in range(2):
        for c in range(CORES):
            for j in range(MINE):
                x = held_ref[verts[(pair * CORES + c) * MINE + j]]
                for part in range(8):
                    o_ref[(part * CORES + c) * 2 + pair, j] = x


def chosen_chunks(verts, held):
    vm = pl.BlockSpec(memory_space=pltpu.VMEM)
    return pl.pallas_call(
        choose,
        out_shape=pltpu.VMEM((8 * CORES * 2, MINE, CH, HD), jnp.bfloat16),
        in_specs=[pl.BlockSpec(memory_space=pltpu.SMEM), vm],
        out_specs=vm,
        name="choose",
        compiler_params=pltpu.CompilerParams(vmem_limit_bytes=SMALL),
    )(in_smem(verts), in_vmem(held))


def lay_out(q_hbm, k_hbm, v_hbm, o_ref, q_ref, k_ref, v_ref, sems):
    step = 8
    copies = [
        pltpu.make_async_copy(k_hbm, k_ref, sems.at[0]),
        pltpu.make_async_copy(v_hbm, v_ref, sems.at[1]),
    ]
    for n, row in enumerate(range(0, ROWS, step)):
        rows = pl.ds(row, step)
        copies.append(pltpu.make_async_copy(q_hbm.at[rows], q_ref.at[rows], sems.at[2 + n]))
    for copy in copies:
        copy.start()
    copies[0].wait()
    copies[1].wait()
    for g in range(GROUPS):
        m = g // 2 * HD
        o_ref[g, :, CHIP_WIDE:WIDE] = (v_ref if g % 2 else k_ref)[:, m : m + HD]
    for n, row in enumerate(range(0, ROWS, step)):
        copies[2 + n].wait()
        for g in range(GROUPS):
            o_ref[g, row : row + step, 0:CHIP_WIDE] = q_ref[
                row : row + step, g * CHIP_WIDE : (g + 1) * CHIP_WIDE
            ]


def pack(q, k, v):
    return pl.pallas_call(
        lay_out,
        out_shape=pltpu.VMEM((GROUPS, ROWS, WIDE), jnp.bfloat16),
        in_specs=[pl.BlockSpec(memory_space=pltpu.HBM)] * 3,
        out_specs=pl.BlockSpec(memory_space=pltpu.VMEM),
        scratch_shapes=[
            pltpu.VMEM((ROWS, QUERY_HEADS * HD), jnp.bfloat16),
            pltpu.VMEM((ROWS, KEY_VALUE_HEADS * HD), jnp.bfloat16),
            pltpu.VMEM((ROWS, KEY_VALUE_HEADS * HD), jnp.bfloat16),
            pltpu.SemaphoreType.DMA((2 + ROWS // 8,)),
        ],
        name="lay_out",
        compiler_params=pltpu.CompilerParams(vmem_limit_bytes=SMALL),
    )(in_hbm(q), in_hbm(k), in_hbm(v))


def to_slots(assign, x_ref, o_ref, sems):
    copies = []
    for k in range(QUERY_HEADS):
        a = assign[k]
        source = (a >> 1 & 1) * GROUPS + (a >> 2)
        lane = pl.ds(pl.multiple_of((a & 1) * HD, HD), HD)
        copies.append(
            pltpu.make_async_copy(
                x_ref.at[source, :, lane], o_ref.at[:, pl.ds(k * HD, HD)], sems.at[k]
            )
        )
        copies[-1].start()
    for copy in copies:
        copy.wait()


def place_slots(assign, x):
    return pl.pallas_call(
        to_slots,
        out_shape=jax.ShapeDtypeStruct((ROWS, QUERY_HEADS * HD), jnp.bfloat16),
        in_specs=[
            pl.BlockSpec(memory_space=pltpu.SMEM),
            pl.BlockSpec(memory_space=pltpu.VMEM),
        ],
        out_specs=pl.BlockSpec(memory_space=pl.ANY),
        scratch_shapes=[pltpu.SemaphoreType.DMA((QUERY_HEADS,))],
        name="to_slots",
        compiler_params=pltpu.CompilerParams(vmem_limit_bytes=SMALL),
    )(in_smem(assign), in_vmem(x))


def per_device(q_rows, k_rows, v_rows, group_assign, vertical_blocks, slash_offsets):
    group = lax.axis_index(HEAD)
    core = lax.axis_index("c")
    odd = lax.axis_index("yb")
    chip = lax.axis_index(("xl", "za", "zb"))
    pair_heads = 2 * CORES * SLOTS
    verts = lax.dynamic_slice_in_dim(vertical_blocks, group // 2 * pair_heads, pair_heads)
    verts = verts.reshape(-1)
    my_head = (group * CORES + core) * SLOTS
    my_verts = lax.dynamic_slice_in_dim(vertical_blocks, my_head, SLOTS).reshape(-1)
    my_offs = lax.dynamic_slice_in_dim(slash_offsets, my_head, SLOTS).reshape(-1)
    place = jnp.stack([chip * CORES * LB, core, odd]).astype(jnp.int32)
    meta = jnp.concatenate([place, my_verts, my_offs])

    sent = pack(q_rows, k_rows, v_rows)
    here = lax.all_to_all(sent, HEAD, 0, 0, tiled=True).reshape(SEQ_ROWS, WIDE)
    here, verts, meta = lax.optimization_barrier((here, verts, meta))
    chunks, x_here = in_chunks(here)
    held = lax.all_to_all(chunks, SEQ, 0, 0, tiled=True)

    other = lax.ppermute(here, "c", [(0, 1), (1, 0)])
    pair = lax.ppermute(x_here, "yb", [(0, 1), (1, 0)])
    diag = lax.ppermute(x_here, ("c", "yb"), [(0, 3), (1, 2), (2, 1), (3, 0)])
    last = last_window(meta, here, other, pair, diag)
    kv_before = lax.ppermute(last, ("xl", "za", "zb"), [(i, i + 1) for i in range(23)])

    spread = chosen_chunks(verts, held.reshape(SUB * PARTS * LB, CH, HD))
    vert = lax.all_to_all(spread, ("xl", "zb", "c", "yb"), 0, 0, tiled=True)
    acc, top, q_here = near(meta, here, other, pair, diag, kv_before)
    out = far(meta, q_here, acc, top, vert.reshape(SUB, 2, MINE, CH, HD))
    back = lax.all_to_all(
        out.reshape(CORES * GROUPS, ROWS, SLOTS * HD), SPLIT, 0, 0, tiled=True
    )
    return place_slots(group_assign, back)


def solution(mesh):
    fine = Mesh(mesh.devices.reshape(2, 3, 4, 2, 2, 4, 2), ALL)
    rows = P(ALL, None)
    return jax.shard_map(
        per_device,
        mesh=fine,
        in_specs=(rows, rows, rows, P(), P(), P()),
        out_specs=rows,
        check_vma=False,
    )
```

```python
import math

import jax
import jax.numpy as jnp
from jax import lax
from jax.experimental import pallas as pl
from jax.experimental.pallas import tpu as pltpu
from jax.sharding import Mesh, PartitionSpec as P


QUERY_HEADS = 64
KEY_VALUE_HEADS = 8
HD = 128
BT = 128
NV = 4
NS = 3
GROUPS = 16
CORES = 2
SLOTS = QUERY_HEADS // GROUPS // CORES
ROWS = 40
SEQ_ROWS = 640
LB = SEQ_ROWS // BT
TOKENS = CORES * SEQ_ROWS
CHIP_WIDE = CORES * SLOTS * HD
WIDE = CHIP_WIDE + HD
MINE = SLOTS * NV
PAIR_SLOTS = 2 * CORES * MINE
CH = 8
PARTS = 3
SUB = 16
ALL = ("xl", "za", "zb", "c", "xh", "ya", "yb")
SEQ = ("xl", "za", "zb", "c")
HEAD = ("xh", "ya", "yb")
SPLIT = ("c", "xh", "ya", "yb")
SCALE = 1.0 / math.sqrt(HD)
NEG = float("-inf")
SMALL = 4 * 1024 * 1024
PAIR = 5
LARGE = 12 * 1024 * 1024


LOG2E_SCALE = SCALE * math.log2(math.e)
DIMS = (((1,), (1,)), ((), ()))


def in_vmem(x):
    return pltpu.with_memory_space_constraint(x, pltpu.VMEM)


def in_smem(x):
    return pltpu.with_memory_space_constraint(x, pltpu.SMEM)


def in_hbm(x):
    return pltpu.with_memory_space_constraint(x, pltpu.HBM)


def both_kinds(meta, here_ref, other_ref, pair_ref, diag_ref):
    own = pl.ds(pl.multiple_of(meta[2] * HD, HD), HD)
    rest = pl.ds(pl.multiple_of((1 - meta[2]) * HD, HD), HD)
    x = slice(CHIP_WIDE, WIDE)
    return ((own, here_ref.at[:, x], other_ref.at[:, x]), (rest, pair_ref, diag_ref))


def near_part(
    meta,
    here_ref,
    other_ref,
    pair_ref,
    diag_ref,
    prev_ref,
    rest_ref,
    acc_hbm,
    top_hbm,
    q_hbm,
    acc_ref,
    top_ref,
    q_ref,
    win,
    kc,
    vc,
    sems,
):
    first_block = meta[0]
    core = meta[1]
    wide = SLOTS * HD
    my_lanes = pl.ds(pl.multiple_of(core * wide, wide), wide)
    mine = pl.multiple_of(core * SEQ_ROWS, SEQ_ROWS)
    theirs = pl.multiple_of((1 - core) * SEQ_ROWS, SEQ_ROWS)
    win[0:SEQ_ROWS, pl.ds(pl.multiple_of(core * HD, HD), HD)] = prev_ref[...]
    win[0:SEQ_ROWS, pl.ds(pl.multiple_of((1 - core) * HD, HD), HD)] = rest_ref[...]
    for lanes, inner, outer in both_kinds(meta, here_ref, other_ref, pair_ref, diag_ref):
        win[pl.ds(SEQ_ROWS + mine, SEQ_ROWS), lanes] = inner[...]
        win[pl.ds(SEQ_ROWS + theirs, SEQ_ROWS), lanes] = outer[...]
    q_ref[pl.ds(mine, SEQ_ROWS), :] = here_ref[:, my_lanes]
    q_ref[pl.ds(theirs, SEQ_ROWS), :] = other_ref[:, my_lanes]
    steps = TOKENS // BT // PAIR
    whole = pltpu.make_async_copy(q_ref, q_hbm, sems.at[2, 0])
    whole.start()

    def put(step):
        rows = pl.ds(pl.multiple_of(step * PAIR * BT, PAIR * BT), PAIR * BT)
        return [
            pltpu.make_async_copy(source.at[rows], target.at[rows], sems.at[n, step])
            for n, (source, target) in enumerate(((acc_ref, acc_hbm), (top_ref, top_hbm)))
        ]

    for i in range(PAIR * SLOTS):
        vc[i, :, HD : 2 * HD] = jnp.ones((NS * BT, HD), jnp.bfloat16)
    causal = lax.broadcasted_iota(jnp.int32, (BT, BT), 0) >= lax.broadcasted_iota(
        jnp.int32, (BT, BT), 1
    )

    def unit(step, carry):
        for i in range(PAIR * SLOTS):
            h = i % SLOTS
            local = step * PAIR + i // SLOTS
            offs = [meta[3 + MINE + h * NS + n] for n in range(NS)]
            good = []
            for n in range(NS):
                at = pl.ds(pl.multiple_of((LB + local - offs[n]) * BT, BT), BT)
                rows = slice(n * BT, (n + 1) * BT)
                kc[i, rows, :] = win[at, 0:HD]
                vc[i, rows, 0:HD] = win[at, HD : 2 * HD]
                good.append(first_block + local - offs[n] >= 0)
            rows = pl.ds(pl.multiple_of(local * BT, BT), BT)
            q = q_ref[rows, h * HD : (h + 1) * HD]
            s = lax.dot_general(q, kc[i], DIMS, preferred_element_type=jnp.float32)
            parts = [jnp.where(causal, s[:, 0:BT], NEG)]
            for n in range(1, NS):
                parts.append(s[:, n * BT : (n + 1) * BT] + jnp.where(good[n], 0.0, NEG))
            top = jnp.maximum(jnp.maximum(parts[0], parts[1]), parts[2])
            top = jnp.broadcast_to(jnp.max(top, axis=1, keepdims=True), (BT, HD))
            w = jnp.concatenate(
                [jnp.exp2((x - top) * LOG2E_SCALE).astype(jnp.bfloat16) for x in parts], axis=1
            )
            acc_ref[rows, 2 * h * HD : 2 * (h + 1) * HD] = jnp.dot(
                w, vc[i], preferred_element_type=jnp.float32
            )
            top_ref[rows, h * HD : (h + 1) * HD] = top
        for copy in put(step):
            copy.start()
        return carry

    lax.fori_loop(0, steps, unit, 0)
    whole.wait()
    for step in range(steps):
        for copy in put(step):
            copy.wait()


def near(meta, here, other, pair, diag, prev, rest):
    vm = pl.BlockSpec(memory_space=pltpu.VMEM)
    return pl.pallas_call(
        near_part,
        out_shape=(
            pltpu.HBM((TOKENS, 2 * SLOTS * HD), jnp.float32),
            pltpu.HBM((TOKENS, SLOTS * HD), jnp.float32),
            pltpu.HBM((TOKENS, SLOTS * HD), jnp.bfloat16),
        ),
        in_specs=[pl.BlockSpec(memory_space=pltpu.SMEM), vm, vm, vm, vm, vm, vm],
        out_specs=tuple(pl.BlockSpec(memory_space=pltpu.HBM) for _ in range(3)),
        scratch_shapes=[
            pltpu.VMEM((TOKENS, 2 * SLOTS * HD), jnp.float32),
            pltpu.VMEM((TOKENS, SLOTS * HD), jnp.float32),
            pltpu.VMEM((TOKENS, SLOTS * HD), jnp.bfloat16),
            pltpu.VMEM((TOKENS + SEQ_ROWS, 2 * HD), jnp.bfloat16),
            pltpu.VMEM((PAIR * SLOTS, NS * BT, HD), jnp.bfloat16),
            pltpu.VMEM((PAIR * SLOTS, NS * BT, 2 * HD), jnp.bfloat16),
            pltpu.SemaphoreType.DMA((3, TOKENS // BT // PAIR)),
        ],
        name="near",
        compiler_params=pltpu.CompilerParams(vmem_limit_bytes=LARGE),
    )(in_smem(meta), *(in_vmem(x) for x in (here, other, pair, diag, prev, rest)))


def far_part(
    meta, q_hbm, acc_hbm, top_hbm, vert_ref, o_ref, q_ref, acc_ref, top_ref, vk, vv, sems
):
    first_block = meta[0]
    steps = TOKENS // BT // PAIR
    moves = ((q_hbm, q_ref), (top_hbm, top_ref), (acc_hbm, acc_ref))

    def fetch(step):
        rows = pl.ds(pl.multiple_of(step * PAIR * BT, PAIR * BT), PAIR * BT)
        return [
            pltpu.make_async_copy(source.at[rows], target.at[rows], sems.at[n, step])
            for n, (source, target) in enumerate(moves)
        ]

    for step in range(steps):
        for copy in fetch(step):
            copy.start()
    for h in range(SLOTS):
        vv[h, :, HD : 2 * HD] = jnp.ones((NV * BT, HD), jnp.bfloat16)
        for n in range(NV):
            rows = slice(n * BT, (n + 1) * BT)
            for kind, target in ((0, vk), (1, vv)):
                x = vert_ref[:, kind, h * NV + n].astype(jnp.float32).reshape(BT, HD)
                target[h, rows, 0:HD] = x.astype(jnp.bfloat16)

    def unit(step, carry):
        moving = fetch(step)
        moving[0].wait()
        moving[1].wait()
        later = []
        both = pl.ds(pl.multiple_of(step * PAIR * BT, PAIR * BT), PAIR * BT)
        for h in range(SLOTS):
            offs = [meta[3 + MINE + h * NS + n] for n in range(NS)]
            verts = [meta[3 + h * NV + n] for n in range(NV)]
            lane = slice(h * HD, (h + 1) * HD)
            s = lax.dot_general(q_ref[both, lane], vk[h], DIMS, preferred_element_type=jnp.float32)
            ws = []
            keeps = []
            for p in range(PAIR):
                local = step * PAIR + p
                block = first_block + local
                parts = []
                for n in range(NV):
                    ok = verts[n] <= block
                    for o in offs:
                        ok = ok & (block - verts[n] != o)
                    for e in range(n):
                        ok = ok & (verts[n] != verts[e])
                    x = s[p * BT : (p + 1) * BT, n * BT : (n + 1) * BT]
                    parts.append(x + jnp.where(ok, 0.0, NEG))
                rows = pl.ds(pl.multiple_of(local * BT, BT), BT)
                old = top_ref[rows, lane]
                top = jnp.maximum(
                    jnp.maximum(parts[0], parts[1]), jnp.maximum(parts[2], parts[3])
                )
                top = jnp.maximum(
                    jnp.broadcast_to(jnp.max(top, axis=1, keepdims=True), (BT, HD)), old
                )
                keeps.append(jnp.exp2((old - top) * LOG2E_SCALE))
                ws.append(
                    jnp.concatenate(
                        [jnp.exp2((x - top) * LOG2E_SCALE).astype(jnp.bfloat16) for x in parts],
                        axis=1,
                    )
                )
            gain = jnp.dot(
                jnp.concatenate(ws, axis=0), vv[h], preferred_element_type=jnp.float32
            )
            later.append((keeps, gain))
        moving[2].wait()
        for h, (keeps, gain) in enumerate(later):
            lane = slice(h * HD, (h + 1) * HD)
            for p in range(PAIR):
                rows = pl.ds(pl.multiple_of((step * PAIR + p) * BT, BT), BT)
                here = slice(p * BT, (p + 1) * BT)
                acc = acc_ref[rows, 2 * h * HD : (2 * h + 1) * HD] * keeps[p] + gain[here, 0:HD]
                total = (
                    acc_ref[rows, (2 * h + 1) * HD : (2 * h + 2) * HD] * keeps[p]
                    + gain[here, HD : 2 * HD]
                )
                o_ref[rows, lane] = (acc / total).astype(jnp.bfloat16)
        return carry

    lax.fori_loop(0, steps, unit, 0)


def far(meta, q, acc, top, vert):
    vm = pl.BlockSpec(memory_space=pltpu.VMEM)
    hbm = pl.BlockSpec(memory_space=pltpu.HBM)
    return pl.pallas_call(
        far_part,
        out_shape=pltpu.VMEM((TOKENS, SLOTS * HD), jnp.bfloat16),
        in_specs=[pl.BlockSpec(memory_space=pltpu.SMEM), hbm, hbm, hbm, vm],
        out_specs=vm,
        scratch_shapes=[
            pltpu.VMEM((TOKENS, SLOTS * HD), jnp.bfloat16),
            pltpu.VMEM((TOKENS, 2 * SLOTS * HD), jnp.float32),
            pltpu.VMEM((TOKENS, SLOTS * HD), jnp.float32),
            pltpu.VMEM((SLOTS, NV * BT, HD), jnp.bfloat16),
            pltpu.VMEM((SLOTS, NV * BT, 2 * HD), jnp.bfloat16),
            pltpu.SemaphoreType.DMA((3, TOKENS // BT // PAIR)),
        ],
        name="far",
        compiler_params=pltpu.CompilerParams(vmem_limit_bytes=LARGE),
    )(in_smem(meta), in_hbm(q), in_hbm(acc), in_hbm(top), in_vmem(vert))


def cut(here_ref, o_hbm, x_ref, one_ref, sems):
    for j in range(LB):
        x = here_ref[j * BT : (j + 1) * BT, CHIP_WIDE:WIDE].astype(jnp.float32)
        for r in range(SUB):
            one_ref[r, j] = x[r * CH : (r + 1) * CH].astype(jnp.bfloat16)
    copies = [
        pltpu.make_async_copy(
            one_ref.at[pl.ds(half * 8, 8)],
            o_hbm.at[pl.ds((half * PARTS + part) * 8, 8)],
            sems.at[half, part],
        )
        for half in range(2)
        for part in range(PARTS)
    ]
    for copy in copies:
        copy.start()
    x_ref[...] = here_ref[:, CHIP_WIDE:WIDE]
    for copy in copies:
        copy.wait()


def in_chunks(here):
    vm = pl.BlockSpec(memory_space=pltpu.VMEM)
    return pl.pallas_call(
        cut,
        out_shape=(
            pltpu.HBM((SUB * PARTS, LB, CH, HD), jnp.bfloat16),
            pltpu.VMEM((SEQ_ROWS, HD), jnp.bfloat16),
        ),
        in_specs=[vm],
        out_specs=(pl.BlockSpec(memory_space=pltpu.HBM), vm),
        scratch_shapes=[
            pltpu.VMEM((SUB, LB, CH, HD), jnp.bfloat16),
            pltpu.SemaphoreType.DMA((2, PARTS)),
        ],
        name="cut",
        compiler_params=pltpu.CompilerParams(vmem_limit_bytes=SMALL),
    )(in_vmem(here))


def newest(meta, here_ref, other_ref, pair_ref, diag_ref, o_ref):
    x = slice(CHIP_WIDE, WIDE)
    core, odd = meta[1], meta[2]
    sources = ((other_ref.at[:, x], diag_ref), (pair_ref, here_ref.at[:, x]))
    for c in range(CORES):
        for parity in range(2):

            @pl.when((core == c) & (odd == parity))
            def _():
                o_ref[...] = sources[c][parity][...]


def half_window(meta, here, other, pair, diag):
    vm = pl.BlockSpec(memory_space=pltpu.VMEM)
    return pl.pallas_call(
        newest,
        out_shape=pltpu.VMEM((SEQ_ROWS, HD), jnp.bfloat16),
        in_specs=[pl.BlockSpec(memory_space=pltpu.SMEM), vm, vm, vm, vm],
        out_specs=vm,
        name="newest",
        compiler_params=pltpu.CompilerParams(vmem_limit_bytes=SMALL),
    )(in_smem(meta), *(in_vmem(x) for x in (here, other, pair, diag)))


def choose(verts, held_ref, o_hbm, one_ref, sems):
    for at in range(PAIR_SLOTS):
        pair, c, j = at // (CORES * MINE), at // MINE % CORES, at % MINE
        one_ref[c * 2 + pair, j] = held_ref[verts[at]]
    copies = [
        pltpu.make_async_copy(one_ref, o_hbm.at[pl.ds(part * 4, 4)], sems.at[part])
        for part in range(8)
    ]
    for copy in copies:
        copy.start()
    for copy in copies:
        copy.wait()


def chosen_chunks(verts, held):
    return pl.pallas_call(
        choose,
        out_shape=pltpu.HBM((8 * CORES * 2, MINE, CH, HD), jnp.bfloat16),
        in_specs=[
            pl.BlockSpec(memory_space=pltpu.SMEM),
            pl.BlockSpec(memory_space=pltpu.VMEM),
        ],
        out_specs=pl.BlockSpec(memory_space=pltpu.HBM),
        scratch_shapes=[
            pltpu.VMEM((CORES * 2, MINE, CH, HD), jnp.bfloat16),
            pltpu.SemaphoreType.DMA((8,)),
        ],
        name="choose",
        compiler_params=pltpu.CompilerParams(vmem_limit_bytes=SMALL),
    )(in_smem(verts), in_vmem(held))


def lay_out(q_hbm, k_hbm, v_hbm, o_hbm, q_ref, k_ref, v_ref, sent, sems):
    step = 8
    spans = [pl.ds(row, step) for row in range(0, ROWS, step)]
    copies = [
        pltpu.make_async_copy(k_hbm, k_ref, sems.at[0]),
        pltpu.make_async_copy(v_hbm, v_ref, sems.at[1]),
    ]
    for n, rows in enumerate(spans):
        copies.append(pltpu.make_async_copy(q_hbm.at[rows], q_ref.at[rows], sems.at[2 + n]))
    for copy in copies:
        copy.start()
    copies[0].wait()
    copies[1].wait()
    for g in range(GROUPS):
        m = g // 2 * HD
        sent[g, :, CHIP_WIDE:WIDE] = (v_ref if g % 2 else k_ref)[:, m : m + HD]
    out = []
    for n, rows in enumerate(spans):
        copies[2 + n].wait()
        for g in range(GROUPS):
            sent[g, rows, 0:CHIP_WIDE] = q_ref[rows, g * CHIP_WIDE : (g + 1) * CHIP_WIDE]
        out.append(
            pltpu.make_async_copy(
                sent.at[:, rows, :], o_hbm.at[:, rows, :], sems.at[2 + len(spans) + n]
            )
        )
        out[-1].start()
    for copy in out:
        copy.wait()


def pack(q, k, v):
    return pl.pallas_call(
        lay_out,
        out_shape=pltpu.HBM((GROUPS, ROWS, WIDE), jnp.bfloat16),
        in_specs=[pl.BlockSpec(memory_space=pltpu.HBM)] * 3,
        out_specs=pl.BlockSpec(memory_space=pltpu.HBM),
        scratch_shapes=[
            pltpu.VMEM((ROWS, QUERY_HEADS * HD), jnp.bfloat16),
            pltpu.VMEM((ROWS, KEY_VALUE_HEADS * HD), jnp.bfloat16),
            pltpu.VMEM((ROWS, KEY_VALUE_HEADS * HD), jnp.bfloat16),
            pltpu.VMEM((GROUPS, ROWS, WIDE), jnp.bfloat16),
            pltpu.SemaphoreType.DMA((2 + 2 * (ROWS // 8),)),
        ],
        name="lay_out",
        compiler_params=pltpu.CompilerParams(vmem_limit_bytes=SMALL),
    )(in_hbm(q), in_hbm(k), in_hbm(v))


def to_slots(assign, x_ref, o_ref, sems):
    copies = []
    for k in range(QUERY_HEADS):
        a = assign[k]
        source = (a >> 1 & 1) * GROUPS + (a >> 2)
        lane = pl.ds(pl.multiple_of((a & 1) * HD, HD), HD)
        copies.append(
            pltpu.make_async_copy(
                x_ref.at[source, :, lane], o_ref.at[:, pl.ds(k * HD, HD)], sems.at[k]
            )
        )
        copies[-1].start()
    for copy in copies:
        copy.wait()


def place_slots(assign, x):
    return pl.pallas_call(
        to_slots,
        out_shape=jax.ShapeDtypeStruct((ROWS, QUERY_HEADS * HD), jnp.bfloat16),
        in_specs=[
            pl.BlockSpec(memory_space=pltpu.SMEM),
            pl.BlockSpec(memory_space=pltpu.VMEM),
        ],
        out_specs=pl.BlockSpec(memory_space=pl.ANY),
        scratch_shapes=[pltpu.SemaphoreType.DMA((QUERY_HEADS,))],
        name="to_slots",
        compiler_params=pltpu.CompilerParams(vmem_limit_bytes=SMALL),
    )(in_smem(assign), in_vmem(x))


def per_device(q_rows, k_rows, v_rows, group_assign, vertical_blocks, slash_offsets):
    group = lax.axis_index(HEAD)
    core = lax.axis_index("c")
    odd = lax.axis_index("yb")
    chip = lax.axis_index(("xl", "za", "zb"))
    pair_heads = 2 * CORES * SLOTS
    verts = lax.dynamic_slice_in_dim(vertical_blocks, group // 2 * pair_heads, pair_heads)
    verts = verts.reshape(-1)
    my_head = (group * CORES + core) * SLOTS
    my_verts = lax.dynamic_slice_in_dim(vertical_blocks, my_head, SLOTS).reshape(-1)
    my_offs = lax.dynamic_slice_in_dim(slash_offsets, my_head, SLOTS).reshape(-1)
    place = jnp.stack([chip * CORES * LB, core, odd]).astype(jnp.int32)
    meta = jnp.concatenate([place, my_verts, my_offs])

    sent = pack(q_rows, k_rows, v_rows)
    here = lax.all_to_all(sent, HEAD, 0, 0, tiled=True).reshape(SEQ_ROWS, WIDE)
    here, verts, meta = lax.optimization_barrier((here, verts, meta))
    chunks, x_here = in_chunks(here)
    held = lax.all_to_all(chunks, SEQ, 0, 0, tiled=True)

    other = lax.ppermute(here, "c", [(0, 1), (1, 0)])
    pair = lax.ppermute(x_here, "yb", [(0, 1), (1, 0)])
    diag = lax.ppermute(x_here, ("c", "yb"), [(0, 3), (1, 2), (2, 1), (3, 0)])
    last = half_window(meta, here, other, pair, diag)
    prev = lax.ppermute(last, ("xl", "za", "zb"), [(i, i + 1) for i in range(23)])
    rest = lax.ppermute(prev, "c", [(0, 1), (1, 0)])

    spread = chosen_chunks(verts, held.reshape(SUB * PARTS * LB, CH, HD))
    vert = lax.all_to_all(spread, ("xl", "zb", "c", "yb"), 0, 0, tiled=True)
    acc, top, q_here = near(meta, here, other, pair, diag, prev, rest)
    out = far(meta, q_here, acc, top, vert.reshape(SUB, 2, MINE, CH, HD))
    back = lax.all_to_all(
        out.reshape(CORES * GROUPS, ROWS, SLOTS * HD), SPLIT, 0, 0, tiled=True
    )
    return place_slots(group_assign, back)


def solution(mesh):
    fine = Mesh(mesh.devices.reshape(2, 3, 4, 2, 2, 4, 2), ALL)
    rows = P(ALL, None)
    return jax.shard_map(
        per_device,
        mesh=fine,
        in_specs=(rows, rows, rows, P(), P(), P()),
        out_specs=rows,
        check_vma=False,
    )
```

```python
import math

import jax
import jax.numpy as jnp
from jax import lax
from jax.experimental import pallas as pl
from jax.experimental.pallas import tpu as pltpu
from jax.sharding import Mesh, PartitionSpec as P


QUERY_HEADS = 64
KEY_VALUE_HEADS = 8
HD = 128
BT = 128
NV = 4
NS = 3
GROUPS = 16
CORES = 2
SLOTS = QUERY_HEADS // GROUPS // CORES
ROWS = 40
SEQ_ROWS = 640
LB = SEQ_ROWS // BT
TOKENS = CORES * SEQ_ROWS
CHIP_WIDE = CORES * SLOTS * HD
WIDE = CHIP_WIDE + HD
MINE = SLOTS * NV
CH = 8
PARTS = 3
SUB = 16
ALL = ("xl", "za", "zb", "c", "xh", "ya", "yb")
SEQ = ("xl", "za", "zb", "c")
HEAD = ("xh", "ya", "yb")
SPLIT = ("c", "xh", "ya", "yb")
SCALE = 1.0 / math.sqrt(HD)
NEG = float("-inf")
SMALL = 4 * 1024 * 1024
PAIR = 10
LARGE = 16 * 1024 * 1024


LOG2E_SCALE = SCALE * math.log2(math.e)
DIMS = (((1,), (1,)), ((), ()))


def in_vmem(x):
    return pltpu.with_memory_space_constraint(x, pltpu.VMEM)


def in_smem(x):
    return pltpu.with_memory_space_constraint(x, pltpu.SMEM)


def in_hbm(x):
    return pltpu.with_memory_space_constraint(x, pltpu.HBM)


def both_kinds(meta, here_ref, other_ref, pair_ref, diag_ref):
    own = pl.ds(pl.multiple_of(meta[2] * HD, HD), HD)
    rest = pl.ds(pl.multiple_of((1 - meta[2]) * HD, HD), HD)
    x = slice(CHIP_WIDE, WIDE)
    return ((own, here_ref.at[:, x], other_ref.at[:, x]), (rest, pair_ref, diag_ref))


def near_part(
    meta,
    here_ref,
    other_ref,
    pair_ref,
    diag_ref,
    prev_ref,
    acc_hbm,
    top_hbm,
    q_hbm,
    acc_ref,
    top_ref,
    q_ref,
    win,
    kc,
    vc,
    sems,
):
    first_block = meta[0]
    core = meta[1]
    wide = SLOTS * HD
    my_lanes = pl.ds(pl.multiple_of(core * wide, wide), wide)
    mine = pl.multiple_of(core * SEQ_ROWS, SEQ_ROWS)
    theirs = pl.multiple_of((1 - core) * SEQ_ROWS, SEQ_ROWS)
    win[0:SEQ_ROWS, :] = prev_ref[...]
    for lanes, inner, outer in both_kinds(meta, here_ref, other_ref, pair_ref, diag_ref):
        win[pl.ds(SEQ_ROWS + mine, SEQ_ROWS), lanes] = inner[...]
        win[pl.ds(SEQ_ROWS + theirs, SEQ_ROWS), lanes] = outer[...]
    q_ref[pl.ds(mine, SEQ_ROWS), :] = here_ref[:, my_lanes]
    q_ref[pl.ds(theirs, SEQ_ROWS), :] = other_ref[:, my_lanes]
    steps = TOKENS // BT // PAIR
    whole = pltpu.make_async_copy(q_ref, q_hbm, sems.at[2, 0])
    whole.start()

    def put(step):
        rows = pl.ds(pl.multiple_of(step * PAIR * BT, PAIR * BT), PAIR * BT)
        return [
            pltpu.make_async_copy(source.at[rows], target.at[rows], sems.at[n, step])
            for n, (source, target) in enumerate(((acc_ref, acc_hbm), (top_ref, top_hbm)))
        ]

    for i in range(PAIR * SLOTS):
        vc[i, :, HD : 2 * HD] = jnp.ones((NS * BT, HD), jnp.bfloat16)
    causal = lax.broadcasted_iota(jnp.int32, (BT, BT), 0) >= lax.broadcasted_iota(
        jnp.int32, (BT, BT), 1
    )

    def unit(step, carry):
        for i in range(PAIR * SLOTS):
            h = i % SLOTS
            local = step * PAIR + i // SLOTS
            offs = [meta[3 + MINE + h * NS + n] for n in range(NS)]
            good = []
            for n in range(NS):
                at = pl.ds(pl.multiple_of((LB + local - offs[n]) * BT, BT), BT)
                rows = slice(n * BT, (n + 1) * BT)
                kc[i, rows, :] = win[at, 0:HD]
                vc[i, rows, 0:HD] = win[at, HD : 2 * HD]
                good.append(first_block + local - offs[n] >= 0)
            rows = pl.ds(pl.multiple_of(local * BT, BT), BT)
            q = q_ref[rows, h * HD : (h + 1) * HD]
            s = lax.dot_general(q, kc[i], DIMS, preferred_element_type=jnp.float32)
            parts = [jnp.where(causal, s[:, 0:BT], NEG)]
            for n in range(1, NS):
                parts.append(s[:, n * BT : (n + 1) * BT] + jnp.where(good[n], 0.0, NEG))
            top = jnp.maximum(jnp.maximum(parts[0], parts[1]), parts[2])
            top = jnp.broadcast_to(jnp.max(top, axis=1, keepdims=True), (BT, HD))
            w = jnp.concatenate(
                [jnp.exp2((x - top) * LOG2E_SCALE).astype(jnp.bfloat16) for x in parts], axis=1
            )
            acc_ref[rows, 2 * h * HD : 2 * (h + 1) * HD] = jnp.dot(
                w, vc[i], preferred_element_type=jnp.float32
            )
            top_ref[rows, h * HD : (h + 1) * HD] = top
        for copy in put(step):
            copy.start()
        return carry

    lax.fori_loop(0, steps, unit, 0)
    whole.wait()
    for step in range(steps):
        for copy in put(step):
            copy.wait()


def near(meta, here, other, pair, diag, prev):
    vm = pl.BlockSpec(memory_space=pltpu.VMEM)
    return pl.pallas_call(
        near_part,
        out_shape=(
            pltpu.HBM((TOKENS, 2 * SLOTS * HD), jnp.float32),
            pltpu.HBM((TOKENS, SLOTS * HD), jnp.float32),
            pltpu.HBM((TOKENS, SLOTS * HD), jnp.bfloat16),
        ),
        in_specs=[pl.BlockSpec(memory_space=pltpu.SMEM), vm, vm, vm, vm, vm],
        out_specs=tuple(pl.BlockSpec(memory_space=pltpu.HBM) for _ in range(3)),
        scratch_shapes=[
            pltpu.VMEM((TOKENS, 2 * SLOTS * HD), jnp.float32),
            pltpu.VMEM((TOKENS, SLOTS * HD), jnp.float32),
            pltpu.VMEM((TOKENS, SLOTS * HD), jnp.bfloat16),
            pltpu.VMEM((TOKENS + SEQ_ROWS, 2 * HD), jnp.bfloat16),
            pltpu.VMEM((PAIR * SLOTS, NS * BT, HD), jnp.bfloat16),
            pltpu.VMEM((PAIR * SLOTS, NS * BT, 2 * HD), jnp.bfloat16),
            pltpu.SemaphoreType.DMA((3, TOKENS // BT // PAIR)),
        ],
        name="near",
        compiler_params=pltpu.CompilerParams(vmem_limit_bytes=LARGE),
    )(in_smem(meta), *(in_vmem(x) for x in (here, other, pair, diag, prev)))


def far_part(
    meta, q_hbm, acc_hbm, top_hbm, vert_ref, o_ref, q_ref, acc_ref, top_ref, vk, vv, sems
):
    first_block = meta[0]
    steps = TOKENS // BT // PAIR
    moves = ((q_hbm, q_ref), (top_hbm, top_ref), (acc_hbm, acc_ref))

    def fetch(step):
        rows = pl.ds(pl.multiple_of(step * PAIR * BT, PAIR * BT), PAIR * BT)
        return [
            pltpu.make_async_copy(source.at[rows], target.at[rows], sems.at[n, step])
            for n, (source, target) in enumerate(moves)
        ]

    for step in range(steps):
        for copy in fetch(step):
            copy.start()
    for h in range(SLOTS):
        vv[h, :, HD : 2 * HD] = jnp.ones((NV * BT, HD), jnp.bfloat16)
        for n in range(NV):
            rows = slice(n * BT, (n + 1) * BT)
            for kind, target in ((0, vk), (1, vv)):
                x = vert_ref[:, kind, h * NV + n].astype(jnp.float32).reshape(BT, HD)
                target[h, rows, 0:HD] = x.astype(jnp.bfloat16)

    def unit(step, carry):
        moving = fetch(step)
        moving[0].wait()
        moving[1].wait()
        later = []
        both = pl.ds(pl.multiple_of(step * PAIR * BT, PAIR * BT), PAIR * BT)
        for h in range(SLOTS):
            offs = [meta[3 + MINE + h * NS + n] for n in range(NS)]
            verts = [meta[3 + h * NV + n] for n in range(NV)]
            lane = slice(h * HD, (h + 1) * HD)
            s = lax.dot_general(q_ref[both, lane], vk[h], DIMS, preferred_element_type=jnp.float32)
            ws = []
            keeps = []
            for p in range(PAIR):
                local = step * PAIR + p
                block = first_block + local
                parts = []
                for n in range(NV):
                    ok = verts[n] <= block
                    for o in offs:
                        ok = ok & (block - verts[n] != o)
                    for e in range(n):
                        ok = ok & (verts[n] != verts[e])
                    x = s[p * BT : (p + 1) * BT, n * BT : (n + 1) * BT]
                    parts.append(x + jnp.where(ok, 0.0, NEG))
                rows = pl.ds(pl.multiple_of(local * BT, BT), BT)
                old = top_ref[rows, lane]
                top = jnp.maximum(
                    jnp.maximum(parts[0], parts[1]), jnp.maximum(parts[2], parts[3])
                )
                top = jnp.maximum(
                    jnp.broadcast_to(jnp.max(top, axis=1, keepdims=True), (BT, HD)), old
                )
                keeps.append(jnp.exp2((old - top) * LOG2E_SCALE))
                ws.append(
                    jnp.concatenate(
                        [jnp.exp2((x - top) * LOG2E_SCALE).astype(jnp.bfloat16) for x in parts],
                        axis=1,
                    )
                )
            gain = jnp.dot(
                jnp.concatenate(ws, axis=0), vv[h], preferred_element_type=jnp.float32
            )
            later.append((keeps, gain))
        moving[2].wait()
        for h, (keeps, gain) in enumerate(later):
            lane = slice(h * HD, (h + 1) * HD)
            for p in range(PAIR):
                rows = pl.ds(pl.multiple_of((step * PAIR + p) * BT, BT), BT)
                here = slice(p * BT, (p + 1) * BT)
                acc = acc_ref[rows, 2 * h * HD : (2 * h + 1) * HD] * keeps[p] + gain[here, 0:HD]
                total = (
                    acc_ref[rows, (2 * h + 1) * HD : (2 * h + 2) * HD] * keeps[p]
                    + gain[here, HD : 2 * HD]
                )
                o_ref[rows, lane] = (acc / total).astype(jnp.bfloat16)
        return carry

    lax.fori_loop(0, steps, unit, 0)


def far(meta, q, acc, top, vert):
    vm = pl.BlockSpec(memory_space=pltpu.VMEM)
    hbm = pl.BlockSpec(memory_space=pltpu.HBM)
    return pl.pallas_call(
        far_part,
        out_shape=pltpu.VMEM((TOKENS, SLOTS * HD), jnp.bfloat16),
        in_specs=[pl.BlockSpec(memory_space=pltpu.SMEM), hbm, hbm, hbm, vm],
        out_specs=vm,
        scratch_shapes=[
            pltpu.VMEM((TOKENS, SLOTS * HD), jnp.bfloat16),
            pltpu.VMEM((TOKENS, 2 * SLOTS * HD), jnp.float32),
            pltpu.VMEM((TOKENS, SLOTS * HD), jnp.float32),
            pltpu.VMEM((SLOTS, NV * BT, HD), jnp.bfloat16),
            pltpu.VMEM((SLOTS, NV * BT, 2 * HD), jnp.bfloat16),
            pltpu.SemaphoreType.DMA((3, TOKENS // BT // PAIR)),
        ],
        name="far",
        compiler_params=pltpu.CompilerParams(vmem_limit_bytes=LARGE),
    )(in_smem(meta), in_hbm(q), in_hbm(acc), in_hbm(top), in_vmem(vert))


def cut(here_ref, o_ref, x_ref):
    x_ref[...] = here_ref[:, CHIP_WIDE:WIDE]
    for j in range(LB):
        x = here_ref[j * BT : (j + 1) * BT, CHIP_WIDE:WIDE].astype(jnp.float32)
        for r in range(SUB):
            chunk = x[r * CH : (r + 1) * CH].astype(jnp.bfloat16)
            for part in range(PARTS):
                o_ref[r // 8 * 8 * PARTS + part * 8 + r % 8, j] = chunk


def in_chunks(here):
    vm = pl.BlockSpec(memory_space=pltpu.VMEM)
    return pl.pallas_call(
        cut,
        out_shape=(
            pltpu.VMEM((SUB * PARTS, LB, CH, HD), jnp.bfloat16),
            pltpu.VMEM((SEQ_ROWS, HD), jnp.bfloat16),
        ),
        in_specs=[vm],
        out_specs=(vm, vm),
        name="cut",
        compiler_params=pltpu.CompilerParams(vmem_limit_bytes=SMALL),
    )(in_vmem(here))


def newest(meta, here_ref, other_ref, pair_ref, diag_ref, o_ref):
    for lanes, inner, outer in both_kinds(meta, here_ref, other_ref, pair_ref, diag_ref):

        @pl.when(meta[1] == 1)
        def _():
            o_ref[:, lanes] = inner[...]

        @pl.when(meta[1] != 1)
        def _():
            o_ref[:, lanes] = outer[...]


def last_window(meta, here, other, pair, diag):
    vm = pl.BlockSpec(memory_space=pltpu.VMEM)
    return pl.pallas_call(
        newest,
        out_shape=pltpu.VMEM((SEQ_ROWS, 2 * HD), jnp.bfloat16),
        in_specs=[pl.BlockSpec(memory_space=pltpu.SMEM), vm, vm, vm, vm],
        out_specs=vm,
        name="newest",
        compiler_params=pltpu.CompilerParams(vmem_limit_bytes=SMALL),
    )(in_smem(meta), *(in_vmem(x) for x in (here, other, pair, diag)))


def choose(verts, held_ref, o_ref):
    for pair in range(2):
        for c in range(CORES):
            for j in range(MINE):
                x = held_ref[verts[(pair * CORES + c) * MINE + j]]
                for part in range(8):
                    o_ref[(part * CORES + c) * 2 + pair, j] = x


def chosen_chunks(verts, held):
    vm = pl.BlockSpec(memory_space=pltpu.VMEM)
    return pl.pallas_call(
        choose,
        out_shape=pltpu.VMEM((8 * CORES * 2, MINE, CH, HD), jnp.bfloat16),
        in_specs=[pl.BlockSpec(memory_space=pltpu.SMEM), vm],
        out_specs=vm,
        name="choose",
        compiler_params=pltpu.CompilerParams(vmem_limit_bytes=SMALL),
    )(in_smem(verts), in_vmem(held))


def lay_out(q_hbm, k_hbm, v_hbm, o_hbm, q_ref, k_ref, v_ref, sent, sems):
    step = 8
    spans = [pl.ds(row, step) for row in range(0, ROWS, step)]
    copies = [
        pltpu.make_async_copy(k_hbm, k_ref, sems.at[0]),
        pltpu.make_async_copy(v_hbm, v_ref, sems.at[1]),
    ]
    for n, rows in enumerate(spans):
        copies.append(pltpu.make_async_copy(q_hbm.at[rows], q_ref.at[rows], sems.at[2 + n]))
    for copy in copies:
        copy.start()
    copies[0].wait()
    copies[1].wait()
    for g in range(GROUPS):
        m = g // 2 * HD
        sent[g, :, CHIP_WIDE:WIDE] = (v_ref if g % 2 else k_ref)[:, m : m + HD]
    out = []
    for n, rows in enumerate(spans):
        copies[2 + n].wait()
        for g in range(GROUPS):
            sent[g, rows, 0:CHIP_WIDE] = q_ref[rows, g * CHIP_WIDE : (g + 1) * CHIP_WIDE]
        out.append(
            pltpu.make_async_copy(
                sent.at[:, rows, :], o_hbm.at[:, rows, :], sems.at[2 + len(spans) + n]
            )
        )
        out[-1].start()
    for copy in out:
        copy.wait()


def pack(q, k, v):
    return pl.pallas_call(
        lay_out,
        out_shape=pltpu.HBM((GROUPS, ROWS, WIDE), jnp.bfloat16),
        in_specs=[pl.BlockSpec(memory_space=pltpu.HBM)] * 3,
        out_specs=pl.BlockSpec(memory_space=pltpu.HBM),
        scratch_shapes=[
            pltpu.VMEM((ROWS, QUERY_HEADS * HD), jnp.bfloat16),
            pltpu.VMEM((ROWS, KEY_VALUE_HEADS * HD), jnp.bfloat16),
            pltpu.VMEM((ROWS, KEY_VALUE_HEADS * HD), jnp.bfloat16),
            pltpu.VMEM((GROUPS, ROWS, WIDE), jnp.bfloat16),
            pltpu.SemaphoreType.DMA((2 + 2 * (ROWS // 8),)),
        ],
        name="lay_out",
        compiler_params=pltpu.CompilerParams(vmem_limit_bytes=SMALL),
    )(in_hbm(q), in_hbm(k), in_hbm(v))


def to_slots(assign, x_ref, o_ref, sems):
    copies = []
    for k in range(QUERY_HEADS):
        a = assign[k]
        source = (a >> 1 & 1) * GROUPS + (a >> 2)
        lane = pl.ds(pl.multiple_of((a & 1) * HD, HD), HD)
        copies.append(
            pltpu.make_async_copy(
                x_ref.at[source, :, lane], o_ref.at[:, pl.ds(k * HD, HD)], sems.at[k]
            )
        )
        copies[-1].start()
    for copy in copies:
        copy.wait()


def place_slots(assign, x):
    return pl.pallas_call(
        to_slots,
        out_shape=jax.ShapeDtypeStruct((ROWS, QUERY_HEADS * HD), jnp.bfloat16),
        in_specs=[
            pl.BlockSpec(memory_space=pltpu.SMEM),
            pl.BlockSpec(memory_space=pltpu.VMEM),
        ],
        out_specs=pl.BlockSpec(memory_space=pl.ANY),
        scratch_shapes=[pltpu.SemaphoreType.DMA((QUERY_HEADS,))],
        name="to_slots",
        compiler_params=pltpu.CompilerParams(vmem_limit_bytes=SMALL),
    )(in_smem(assign), in_vmem(x))


def per_device(q_rows, k_rows, v_rows, group_assign, vertical_blocks, slash_offsets):
    group = lax.axis_index(HEAD)
    core = lax.axis_index("c")
    odd = lax.axis_index("yb")
    chip = lax.axis_index(("xl", "za", "zb"))
    pair_heads = 2 * CORES * SLOTS
    verts = lax.dynamic_slice_in_dim(vertical_blocks, group // 2 * pair_heads, pair_heads)
    verts = verts.reshape(-1)
    my_head = (group * CORES + core) * SLOTS
    my_verts = lax.dynamic_slice_in_dim(vertical_blocks, my_head, SLOTS).reshape(-1)
    my_offs = lax.dynamic_slice_in_dim(slash_offsets, my_head, SLOTS).reshape(-1)
    place = jnp.stack([chip * CORES * LB, core, odd]).astype(jnp.int32)
    meta = jnp.concatenate([place, my_verts, my_offs])

    sent = pack(q_rows, k_rows, v_rows)
    here = lax.all_to_all(sent, HEAD, 0, 0, tiled=True).reshape(SEQ_ROWS, WIDE)
    here, verts, meta = lax.optimization_barrier((here, verts, meta))
    chunks, x_here = in_chunks(here)
    held = lax.all_to_all(chunks, SEQ, 0, 0, tiled=True)

    other = lax.ppermute(here, "c", [(0, 1), (1, 0)])
    pair = lax.ppermute(x_here, "yb", [(0, 1), (1, 0)])
    diag = lax.ppermute(x_here, ("c", "yb"), [(0, 3), (1, 2), (2, 1), (3, 0)])
    last = last_window(meta, here, other, pair, diag)
    kv_before = lax.ppermute(last, ("xl", "za", "zb"), [(i, i + 1) for i in range(23)])

    spread = chosen_chunks(verts, held.reshape(SUB * PARTS * LB, CH, HD))
    vert = lax.all_to_all(spread, ("xl", "zb", "c", "yb"), 0, 0, tiled=True)
    acc, top, q_here = near(meta, here, other, pair, diag, kv_before)
    out = far(meta, q_here, acc, top, vert.reshape(SUB, 2, MINE, CH, HD))
    back = lax.all_to_all(
        out.reshape(CORES * GROUPS, ROWS, SLOTS * HD), SPLIT, 0, 0, tiled=True
    )
    return place_slots(group_assign, back)


def solution(mesh):
    fine = Mesh(mesh.devices.reshape(2, 3, 4, 2, 2, 4, 2), ALL)
    rows = P(ALL, None)
    return jax.shard_map(
        per_device,
        mesh=fine,
        in_specs=(rows, rows, rows, P(), P(), P()),
        out_specs=rows,
        check_vma=False,
    )
```
